256 devices in a mesh: ctx: 16 (over y, x), exp: 16 (over z, core).
Axes of the slice: x: 4, y: 4, z: 8, core: 2. Of those that a mesh axis runs over, the one named last changes fastest.
Arguments:
- tokens: bfloat16 [2048, 4096], P('ctx', 'exp'), may hold values from -6 to 6
- input_weight: bfloat16 [4096, 8192], P('ctx', 'exp'), may hold values from -0.09375 to 0.09375
- gate_weight: bfloat16 [4096, 8192], P('ctx', 'exp'), may hold values from -0.09375 to 0.09375
- conv_weight: float32 [4, 8192], P(None, 'exp'), may hold values from -3 to 3
- conv_bias: float32 [8192], P('exp'), may hold values from -3 to 3
- state_weight: bfloat16 [8192, 32], P('exp'), may hold values from -0.0078125 to 0.0078125
- step_size: float32 [2048, 8192], P('ctx', 'exp'), may hold values from 0 to 1, as said below
- skip_gain: float32 [8192], P('exp'), may hold values from 0.5 to 2
- output_weight: bfloat16 [8192, 4096], P('exp', 'ctx'), may hold values from -0.0625 to 0.0625
- norm_gain: float32 [4096], replicated, may hold values from 0.1 to 1.9
- router_weight: bfloat16 [4096, 16], replicated, may hold values from -0.09375 to 0.09375
- expert_gate: bfloat16 [16, 7168, 4096], P('exp', 'ctx'), may hold values from -0.09375 to 0.09375
- expert_up: bfloat16 [16, 7168, 4096], P('exp', 'ctx'), may hold values from -0.09375 to 0.09375
- expert_down: bfloat16 [16, 7168, 4096], P('exp', 'ctx'), may hold values from -0.0625 to 0.0625
- expert_ids: int32 [2048, 2], P(('ctx', 'exp')), may hold values from 0 to 15, all different within a row; in each aligned block of 8 rows (0 to 7, 8 to 15, ...) at most 2 rows name the same one
Outputs:
- layer_out: bfloat16 [2048, 4096], P(('ctx', 'exp'))
The draws below stay inside these ranges and needn't reach their ends.
Inputs may be any that keep to these rules, and one draw needn't show every extreme that they name: `expert_ids`: each token names 2 different experts; in each aligned block of 8 tokens no expert is named by more than 2 tokens. `step_size`: a positive rate for each token and channel.
All inputs are finite; a program needn't handle non-finite values.
Results may differ from the reference program's by a relative error of at most 0.028.
Values may be sent and summed in bfloat16 or wider, within the bound.
A program may use at most 128 MiB of HBM per device.

```python
import math
import jax
import jax.numpy as jnp
import numpy as np
from jax import lax

D = 4096
INNER_CHANNELS = 8192
STATE = 16
CONV = 4
EF = 7168
TOP = 2
CAP = 2
STRETCH = 128
EXPERTS = 16
TEXT_LEN_ITEMS = 2048
ROWS = 8
N_EXP = 16


def draw_step_size(key, part):
    divided_seed_handles = jax.random.split(key, 7)
    slow_share = 0.5
    is_slow = jax.random.bernoulli(divided_seed_handles[0], slow_share, (INNER_CHANNELS,))
    slow_rate = jnp.exp(jax.random.uniform(divided_seed_handles[1], (INNER_CHANNELS,), jnp.float32, math.log(0.08), math.log(0.5))) / TEXT_LEN_ITEMS
    fast_rate = jnp.exp(jax.random.uniform(divided_seed_handles[2], (INNER_CHANNELS,), jnp.float32, math.log(1.0 / 50.0), math.log(1.0 / 30.0)))
    baseline_rate = jnp.where(is_slow, slow_rate, fast_rate)
    jaggedness = jnp.exp(jax.random.uniform(divided_seed_handles[3], (TEXT_LEN_ITEMS, INNER_CHANNELS), jnp.float32, math.log(0.5), math.log(2.0)))
    phase_shift = jax.random.uniform(divided_seed_handles[4], (), jnp.float32, 0.0, 2.0 * math.pi)
    along_sequence = jnp.arange(TEXT_LEN_ITEMS, dtype=jnp.float32) / TEXT_LEN_ITEMS
    position_multiplier = jnp.exp(0.7 * jnp.sin(6.0 * math.pi * along_sequence + phase_shift))
    surge_onset_index = jax.random.randint(divided_seed_handles[5], (2,), 0, TEXT_LEN_ITEMS)
    surge_entries = jnp.any(jnp.arange(TEXT_LEN_ITEMS, dtype=jnp.int32)[:, None] == surge_onset_index[None, :], 1).astype(jnp.float32)
    spike_length = jax.random.uniform(divided_seed_handles[6], (TEXT_LEN_ITEMS, INNER_CHANNELS), jnp.float32, math.log(1.25), math.log(2.0))
    return baseline_rate[None, :] * jaggedness * position_multiplier[:, None] + surge_entries[:, None] * spike_length


def levels(stream_key, shape, shards, smallest, high):
    factor_of, own = 1.0, jax.random.fold_in(stream_key, 6)
    for axis_at, shards_of in shards:
        heights = jnp.exp(jax.random.uniform(jax.random.fold_in(own, axis_at), (shards_of,), jnp.float32, smallest / len(shards), high / len(shards)))
        factor_of = factor_of * jnp.repeat(heights, shape[axis_at] // shards_of).reshape([-1 if axis == axis_at else 1 for axis in range(len(shape))])
    return factor_of


def shared_out(own_key, own, number, rows, number_of, top, bound, lean):
    ranking = jax.random.permutation(own_key, number_of)
    packed, usual = load_shares(number_of, rows * top, bound, lean, True), load_shares(number_of, rows * top, bound, lean, False)
    places = jnp.arange(number_of)

    def named(sizes, turn):
        used = int((sizes > 0).sum())
        fixed = max(1, used // 4)
        moved = fixed + (places - fixed + turn * (used - fixed)) % max(1, number_of - fixed)
        return jnp.zeros((number_of,), jnp.int32).at[ranking[jnp.where(places < fixed, places, moved)]].set(jnp.asarray(sizes, jnp.int32))

    sizes = jnp.where(number % 4 == 0, named(packed, number // 4), named(usual, number - number // 4 - 1))
    mixed = jax.random.permutation(jax.random.fold_in(own, 3), number_of)
    giver, taker = mixed[0:number_of // 2 * 2:2], mixed[1:number_of // 2 * 2:2]
    margin = jnp.minimum(sizes[giver] - 1, bound - sizes[taker]) // 2
    margin = jnp.where((giver == ranking[0]) | (taker == ranking[0]) | (sizes[taker] == 0), 0, jnp.maximum(margin, 0))
    moved = jax.random.randint(jax.random.fold_in(own, 4), (number_of // 2,), 0, 1 << 20) % (margin + 1)
    sizes = sizes.at[giver].add(-moved).at[taker].add(moved)
    labels = jnp.searchsorted(jnp.cumsum(sizes), jnp.arange(rows * top), side="right").astype(jnp.int32)
    listing = labels.reshape(top, rows).T
    listing = listing[jax.random.permutation(jax.random.fold_in(own, 1), rows)]
    turn = jax.random.randint(jax.random.fold_in(own, 2), (rows, 1), 0, top)
    return jnp.take_along_axis(listing, (jnp.arange(top)[None, :] + turn) % top, axis=1)


def load_shares(count, total, most, lean, full):
    loads = [(1 << 20) // math.isqrt(rank ** lean) + 1 for rank in range(1, count + 1)]
    largest = most if full else min(most, max(-(-total // count), total * loads[0] // sum(loads)))
    least = 1 if total - largest >= count - 1 else 0
    counts, rest = [largest] + [least] * (count - 1), total - largest - least * (count - 1)
    while rest > 0:
        candidates = [i for i in range(1, count) if counts[i] < largest] or [i for i in range(1, count) if counts[i] < most]
        pool, budget = sum([loads[i] for i in candidates]), rest
        for i in candidates:
            more = min(most - counts[i], max(1, budget * loads[i] // pool), rest)
            counts[i] = counts[i] + more
            rest = rest - more
    return np.array(counts)


def noise(stream_key, extent, deviation, bound, shards=(), held_as=jnp.bfloat16):
    factor_of = levels(stream_key, extent, shards, -0.22, 0.18) if shards else 1.0
    array = jax.random.normal(stream_key, extent, jnp.float32) * deviation * factor_of
    return jnp.minimum(jnp.maximum(array, -bound), bound).astype(held_as)


def setup_inputs(seed: int = 0) -> dict:
    key_list = jax.random.split(jax.random.key(seed), 16)
    tokens = noise(key_list[0], (TEXT_LEN_ITEMS, D), 1.0, 6.0, ((0, 16), (1, 16)))
    input_weight = noise(key_list[1], (D, INNER_CHANNELS), D ** -0.5, 0.09375, ((0, 16), (1, 16)))
    gate_weight = noise(key_list[2], (D, INNER_CHANNELS), D ** -0.5, 0.09375, ((0, 16), (1, 16)))
    conv_weight = noise(key_list[3], (CONV, INNER_CHANNELS), 0.5, 3.0, ((1, 16),), jnp.float32)
    conv_bias = noise(key_list[4], (INNER_CHANNELS,), 0.5, 3.0, ((0, 16),), jnp.float32)
    state_weight = noise(key_list[5], (INNER_CHANNELS, 2 * STATE), (64 * INNER_CHANNELS) ** -0.5, 0.0078125, ((0, 16),))
    step_size = draw_step_size(jax.random.fold_in(key_list[15], 71), 0)
    skip_gain = jnp.clip(0.5 + 1.5 * jax.random.uniform(key_list[7], (INNER_CHANNELS,), jnp.float32) ** levels(key_list[7], (INNER_CHANNELS,), ((0, 16),), -0.2, 0.2), 0.5, 2.0)
    output_weight = noise(key_list[8], (INNER_CHANNELS, D), INNER_CHANNELS ** -0.5, 0.0625, ((0, 16), (1, 16)))
    norm_gain = jnp.clip(1.0 + 0.18 * jax.random.normal(key_list[9], (D,), jnp.float32), 0.1, 1.9)
    router_weight = noise(key_list[10], (D, EXPERTS), D ** -0.5, 0.09375)
    expert_gate = noise(key_list[11], (EXPERTS, EF, D), D ** -0.5, 0.09375, ((0, 16), (1, 16)))
    expert_up = noise(key_list[12], (EXPERTS, EF, D), D ** -0.5, 0.09375, ((0, 16), (1, 16)))
    expert_down = noise(key_list[13], (EXPERTS, EF, D), EF ** -0.5, 0.0625, ((0, 16), (1, 16)))
    expert_ids_keys = jax.random.split(jax.random.fold_in(key_list[14], 1), TEXT_LEN_ITEMS // (STRETCH // N_EXP))
    expert_ids_turns = jax.random.permutation(jax.random.fold_in(key_list[14], 3), TEXT_LEN_ITEMS // (STRETCH // N_EXP))
    expert_ids = jax.vmap(lambda own, number: shared_out(jax.random.fold_in(key_list[14], 2), own, number, STRETCH // N_EXP, EXPERTS, TOP, CAP, 2))(expert_ids_keys, expert_ids_turns).reshape((TEXT_LEN_ITEMS, TOP))
    return {"tokens": tokens, "input_weight": input_weight, "gate_weight": gate_weight, "conv_weight": conv_weight, "conv_bias": conv_bias, "state_weight": state_weight, "step_size": step_size, "skip_gain": skip_gain, "output_weight": output_weight, "norm_gain": norm_gain, "router_weight": router_weight, "expert_gate": expert_gate, "expert_up": expert_up, "expert_down": expert_down, "expert_ids": expert_ids}


precise = lax.Precision.HIGHEST

def reference(tokens, input_weight, gate_weight, conv_weight, conv_bias, state_weight, step_size, skip_gain, output_weight, norm_gain, router_weight, expert_gate, expert_up, expert_down, expert_ids):
    inner_x = jnp.dot(tokens, input_weight, preferred_element_type=jnp.float32).astype(jnp.bfloat16)
    inner_z = jnp.dot(tokens, gate_weight, preferred_element_type=jnp.float32).astype(jnp.bfloat16)
    extended = jnp.concatenate([jnp.zeros((CONV - 1, INNER_CHANNELS), jnp.bfloat16), inner_x], 0).astype(jnp.float32)
    filtered = jnp.broadcast_to(conv_bias[None, :], (TEXT_LEN_ITEMS, INNER_CHANNELS))
    for offset in range(CONV):
        filtered = filtered + conv_weight[offset][None, :] * extended[offset:offset + TEXT_LEN_ITEMS]
    mixer_in = jax.nn.silu(filtered).astype(jnp.bfloat16)
    mixer_wide = mixer_in.astype(jnp.float32)
    projections = jnp.dot(mixer_in, state_weight, preferred_element_type=jnp.float32)
    input_gain = projections[:, :STATE]
    readout = projections[:, STATE:]
    keep_rate = jnp.exp(-step_size)

    def advance(state, inputs):
        keep_row, incoming_vector, gain_row, read_row = inputs
        state = keep_row[:, None] * state + incoming_vector[:, None] * gain_row[None, :]
        return (state, jnp.dot(state, read_row, precision=precise))
    empty_state = jnp.zeros((INNER_CHANNELS, STATE), jnp.float32)
    readings = lax.scan(advance, empty_state, (keep_rate, mixer_wide, input_gain, readout))[1]
    mixed_state = (readings + skip_gain[None, :] * mixer_wide) * jax.nn.silu(inner_z.astype(jnp.float32))
    blender_result = mixed_state.astype(jnp.bfloat16)
    projected = jnp.dot(blender_result, output_weight, preferred_element_type=jnp.float32)
    residual = (tokens.astype(jnp.float32) + projected).astype(jnp.bfloat16)
    stream = residual.astype(jnp.float32)
    normed = (stream * lax.rsqrt(lax.optimization_barrier(jnp.mean(stream * stream, -1, keepdims=True)) + 1e-05) * norm_gain[None, :]).astype(jnp.bfloat16)
    logits = jnp.dot(normed, router_weight, preferred_element_type=jnp.float32)
    chosen = expert_ids[:, :, None] == jnp.arange(EXPERTS, dtype=jnp.int32)[None, None, :]
    selected_entry = lax.optimization_barrier(jnp.sum(jnp.where(chosen, logits[:, None, :], 0.0), -1))
    shares = jax.nn.sigmoid(selected_entry - selected_entry[:, ::-1])
    slot_bound = CAP * (TEXT_LEN_ITEMS // ROWS)
    positions = jnp.arange(slot_bound, dtype=jnp.int32)

    def one_expert(totals, expert):
        routed = expert_ids == expert
        present = jnp.any(routed, 1)
        weight = lax.optimization_barrier(jnp.sum(jnp.where(routed, shares, 0.0), 1))
        token_index = jnp.nonzero(present, size=slot_bound, fill_value=0)[0].astype(jnp.int32)
        valid_slot = positions < jnp.sum(present.astype(jnp.int32))
        rows_in = normed[token_index].astype(jnp.float32)
        gate_value = jnp.dot(rows_in, expert_gate[expert].astype(jnp.float32).T, precision=precise)
        up_value = jnp.dot(rows_in, expert_up[expert].astype(jnp.float32).T, precision=precise)
        hidden = (jax.nn.silu(gate_value) * up_value).astype(jnp.bfloat16)
        output = jnp.dot(hidden.astype(jnp.float32), expert_down[expert].astype(jnp.float32), precision=precise).astype(jnp.bfloat16)
        weighted = jnp.where(valid_slot[:, None], weight[token_index][:, None] * output.astype(jnp.float32), 0.0)
        return (totals.at[token_index].add(weighted), None)
    moe_out = lax.scan(one_expert, jnp.zeros((TEXT_LEN_ITEMS, D), jnp.float32), jnp.arange(EXPERTS, dtype=jnp.int32))[0]
    return (stream + moe_out).astype(jnp.bfloat16)
```

```python
import jax
import jax.numpy as jnp
from jax import lax
from jax.sharding import PartitionSpec as P

STATE = 16
CONV = 4
TOP = 2
CAP = 2


precise = lax.Precision.HIGHEST


def shifted(shard, axis, by):
    devices = lax.axis_size(axis)
    pairs = [(i, i + by) for i in range(devices) if 0 <= i + by < devices]
    return lax.ppermute(shard, axis, pairs)


def running_sum(values):
    length = values.shape[0]
    lower = jnp.tril(jnp.ones((length, length), jnp.float32))
    return jnp.dot(lower, values, precision=precise)


def causal_part(scores, decay_block, input_block):
    length = decay_block.shape[0]
    causal = (jnp.arange(length)[:, None] >= jnp.arange(length)[None, :])[:, :, None]
    distance = decay_block[:, None, :] - decay_block[None, :, :]
    weight = jnp.where(causal, jnp.exp(-jnp.where(causal, distance, 0.0)), 0.0)
    return jnp.einsum("ts,tsc,sc->tc", scores, weight, input_block, precision=precise)


def local(
    tokens,
    input_weight,
    gate_weight,
    conv_weight,
    conv_bias,
    state_weight,
    step_size,
    skip_gain,
    output_weight,
    norm_gain,
    router_weight,
    expert_gate,
    expert_up,
    expert_down,
    expert_ids,
):
    whole_stretch = lax.all_gather(tokens, "exp", axis=1, tiled=True)
    stretch_rows = whole_stretch.shape[0]
    inner_width = input_weight.shape[1]
    inner_x = jnp.dot(
        whole_stretch,
        lax.all_gather(input_weight, "ctx", axis=0, tiled=True),
        preferred_element_type=jnp.float32,
    )
    inner_z = jnp.dot(
        whole_stretch,
        lax.all_gather(gate_weight, "ctx", axis=0, tiled=True),
        preferred_element_type=jnp.float32,
    )
    inner_x = inner_x.astype(jnp.bfloat16)
    inner_z = inner_z.astype(jnp.bfloat16)
    earlier_rows = shifted(inner_x[stretch_rows - (CONV - 1) :], "ctx", 1)
    extended = jnp.concatenate([earlier_rows, inner_x], 0).astype(jnp.float32)
    filtered = jnp.broadcast_to(conv_bias[None, :], (stretch_rows, inner_width))
    for offset in range(CONV):
        filtered = (
            filtered + conv_weight[offset][None, :] * extended[offset : offset + stretch_rows]
        )
    mixer_in = jax.nn.silu(filtered).astype(jnp.bfloat16)
    mixer_wide = mixer_in.astype(jnp.float32)
    projections = lax.psum(
        jnp.dot(mixer_in, state_weight, preferred_element_type=jnp.float32), "exp"
    )
    input_gain = projections[:, :STATE]
    readout = projections[:, STATE:]
    cumulative = running_sum(step_size)
    scores = jnp.dot(readout, input_gain.T, precision=precise)
    block_width = 128
    block_count = inner_width // block_width
    decay_blocks = cumulative.reshape(stretch_rows, block_count, block_width).transpose(1, 0, 2)
    incoming_slabs = mixer_wide.reshape(stretch_rows, block_count, block_width).transpose(1, 0, 2)
    inside = lax.map(
        lambda paired: causal_part(scores, paired[0], paired[1]), (decay_blocks, incoming_slabs)
    )
    inside = inside.transpose(1, 0, 2).reshape(stretch_rows, inner_width)
    total_decay = cumulative[stretch_rows - 1]
    tail_weight = jnp.exp(-(total_decay[None, :] - cumulative)) * mixer_wide
    local_end = jnp.dot(tail_weight.T, input_gain, precision=precise)
    stretch_keep = jnp.exp(-total_decay)

    def relay_step(turn_index, received):
        leaving = stretch_keep[:, None] * received + local_end
        return shifted(leaving, "ctx", 1)

    entering = lax.fori_loop(0, lax.axis_size("ctx") - 1, relay_step, jnp.zeros_like(local_end))
    carried = jnp.exp(-cumulative) * jnp.dot(readout, entering.T, precision=precise)
    mixed_state = (inside + carried + skip_gain[None, :] * mixer_wide) * jax.nn.silu(
        inner_z.astype(jnp.float32)
    )
    blender_result = mixed_state.astype(jnp.bfloat16)
    row_count = expert_ids.shape[0]
    start_row = lax.axis_index("exp") * row_count
    own_tokens = lax.dynamic_slice_in_dim(whole_stretch, start_row, row_count, 0)
    out_whole = lax.all_gather(output_weight, "ctx", axis=1, tiled=True)
    projected = lax.psum_scatter(
        jnp.dot(blender_result, out_whole, preferred_element_type=jnp.float32).astype(jnp.bfloat16),
        "exp",
        scatter_dimension=0,
        tiled=True,
    ).astype(jnp.float32)
    residual = (own_tokens.astype(jnp.float32) + projected).astype(jnp.bfloat16)
    stream = residual.astype(jnp.float32)
    normed = (
        stream
        * lax.rsqrt(jnp.mean(stream * stream, -1, keepdims=True) + 1e-05)
        * norm_gain[None, :]
    ).astype(jnp.bfloat16)
    logits = jnp.dot(normed, router_weight, preferred_element_type=jnp.float32)
    experts = router_weight.shape[1]
    expert_range = jnp.arange(experts, dtype=jnp.int32)
    chosen = expert_ids[:, :, None] == expert_range[None, None, :]
    selected_entry = jnp.sum(jnp.where(chosen, logits[:, None, :], 0.0), -1)
    shares = jax.nn.sigmoid(selected_entry - selected_entry[:, ::-1])
    flat_hits = chosen.reshape(row_count * TOP, experts).astype(jnp.int32)
    earlier_hits = jnp.dot(
        jnp.tril(jnp.ones((row_count * TOP, row_count * TOP), jnp.float32), -1),
        flat_hits.astype(jnp.float32),
        precision=precise,
    ).astype(jnp.int32)
    slot_index = jnp.sum(earlier_hits * flat_hits, -1)
    target = expert_ids.reshape(-1) * CAP + slot_index
    placed = target[:, None] == jnp.arange(experts * CAP, dtype=jnp.int32)[None, :]
    placed = placed.reshape(row_count, TOP, experts * CAP)
    selector = jnp.any(placed, 1).astype(jnp.bfloat16)
    outgoing = lax.dot_general(
        selector, normed, (((0,), (0,)), ((), ())), preferred_element_type=jnp.float32
    ).astype(jnp.bfloat16)
    outgoing = outgoing.reshape(experts, CAP, -1)
    arrived = lax.all_to_all(outgoing, "exp", split_axis=0, concat_axis=0, tiled=True)
    arrived = arrived.reshape(-1, arrived.shape[2])
    gate_part = expert_gate[0]
    up_part = expert_up[0]
    down_part = expert_down[0]
    shard_rows = lax.all_gather(arrived, "ctx", axis=0, tiled=True)
    gate_value = lax.dot_general(
        shard_rows, gate_part, (((1,), (1,)), ((), ())), preferred_element_type=jnp.float32
    )
    up_value = lax.dot_general(
        shard_rows, up_part, (((1,), (1,)), ((), ())), preferred_element_type=jnp.float32
    )
    hidden = (jax.nn.silu(gate_value) * up_value).astype(jnp.bfloat16)
    partial_out = jnp.dot(hidden, down_part, preferred_element_type=jnp.float32)
    finished = lax.psum_scatter(
        partial_out.astype(jnp.bfloat16), "ctx", scatter_dimension=0, tiled=True
    )
    returned = lax.all_to_all(
        finished.reshape(experts, CAP, -1), "exp", split_axis=0, concat_axis=0, tiled=True
    )
    returned = returned.reshape(experts * CAP, -1).astype(jnp.float32)
    combine = jnp.sum(jnp.where(placed, shares[:, :, None], 0.0), 1)
    moe_out = jnp.dot(combine, returned, precision=precise)
    return (stream + moe_out).astype(jnp.bfloat16)


def solution(mesh):
    in_specs = (
        P("ctx", "exp"),
        P("ctx", "exp"),
        P("ctx", "exp"),
        P(None, "exp"),
        P("exp"),
        P("exp", None),
        P("ctx", "exp"),
        P("exp"),
        P("exp", "ctx"),
        P(),
        P(),
        P("exp", "ctx", None),
        P("exp", "ctx", None),
        P("exp", "ctx", None),
        P(("ctx", "exp"), None),
    )
    out_specs = P(("ctx", "exp"), None)
    return jax.shard_map(local, mesh=mesh, in_specs=in_specs, out_specs=out_specs, check_vma=False)
```

```python
import functools

import jax
import jax.numpy as jnp
from jax import lax
from jax.experimental import pallas as pl
from jax.experimental.pallas import tpu as pltpu
from jax.sharding import PartitionSpec as P

STATE = 16
CONV = 4
TOP = 2
CAP = 2
SIDE = 4
PLANE = SIDE * SIDE
DEPTH = 8
EXPS = 2 * DEPTH
CHUNK = 8

precise = lax.Precision.HIGHEST
f32 = jnp.float32
bf16 = jnp.bfloat16
MESH = pl.DeviceIdType.MESH


def remote(src, dst, send_sem, recv_sem, device):
    return pltpu.make_async_remote_copy(
        src_ref=src,
        dst_ref=dst,
        send_sem=send_sem,
        recv_sem=recv_sem,
        device_id=device,
        device_id_type=MESH,
    )


def greet(ctx_peers, exp_peers):
    c, e = lax.axis_index("ctx"), lax.axis_index("exp")
    barrier = pltpu.get_barrier_semaphore()
    count = 0
    if ctx_peers:

        @pl.loop(1, PLANE)
        def _(d):
            pl.semaphore_signal(
                barrier, inc=1, device_id=(lax.rem(c + d, PLANE), e), device_id_type=MESH
            )

        count += PLANE - 1
    if exp_peers:

        @pl.loop(1, EXPS)
        def _(d):
            pl.semaphore_signal(
                barrier, inc=1, device_id=(c, lax.rem(e + d, EXPS)), device_id_type=MESH
            )

        count += EXPS - 1
    pl.semaphore_wait(barrier, count)


class PlaneView:
    def __init__(self, x_first):
        c, self.e = lax.axis_index("ctx"), lax.axis_index("exp")
        y, x = c // SIDE, lax.rem(c, SIDE)
        self.x_first = x_first
        self.f, self.s = (x, y) if x_first else (y, x)

    def at(self, df, ds):
        f, s = lax.rem(self.f + df + SIDE, SIDE), lax.rem(self.s + ds + SIDE, SIDE)
        return s * SIDE + f if self.x_first else f * SIDE + s


class PlaneGather:
    ORDER = (0, -1, 1, 2)

    def __init__(self, part, x_first, send, recv):
        self.view, self.part, self.send, self.recv = PlaneView(x_first), part, send, recv

    def copy(self, k, slot, which, target):
        block = self.part(slot, which)
        return remote(block, block, self.send.at[k], self.recv.at[k], (target, self.view.e))

    def sent(self, k):
        at = self.view.at
        if k < 4:
            slot, which = ((0, None), (0, None), (-1, 0), (1, 1))[k]
            return self.copy(k, at(slot, 0), which, at(1 if k % 2 == 0 else -1, 0))
        df, kind = self.ORDER[(k - 4) // 4], (k - 4) % 4
        slot, which = ((0, None), (0, None), (-1, 0), (1, 1))[kind]
        return self.copy(k, at(df, slot), which, at(0, 1 if kind % 2 == 0 else -1))

    def arrived(self, k):
        at = self.view.at
        if k < 4:
            slot, which = ((-1, None), (1, None), (2, 0), (2, 1))[k]
            return self.copy(k, at(slot, 0), which, at(0, 0))
        df, kind = self.ORDER[(k - 4) // 4], (k - 4) % 4
        slot, which = ((-1, None), (1, None), (2, 0), (2, 1))[kind]
        return self.copy(k, at(df, slot), which, at(0, 0))

    def start(self, *ks):
        for k in ks:
            self.sent(k).start()

    def await_(self, *ks):
        for k in ks:
            self.arrived(k).wait_recv()

    def finish(self):
        for k in range(20):
            self.sent(k).wait_send()


def first_sends(gathers):
    for g in gathers:
        g.start(0, 1)
    for g in gathers:
        g.start(4, 5)


def first_hop(gathers):
    for g in gathers:
        g.await_(0)
        g.start(2, 8, 9)
        g.await_(1)
        g.start(3, 12, 13)


def first_axis_done(gathers):
    for g in gathers:
        g.await_(2, 3)
        g.start(16, 17)


def second_hop(gathers):
    for j in range(4):
        for g in gathers:
            g.await_(4 + 4 * j)
            g.start(6 + 4 * j)
            g.await_(5 + 4 * j)
            g.start(7 + 4 * j)


def second_axis_done(gathers):
    for j in range(4):
        for g in gathers:
            g.await_(6 + 4 * j, 7 + 4 * j)


def rows_part(ref, begin, length):
    def part(slot, which):
        if which is None:
            return ref.at[slot, pl.ds(begin, length), :]
        return ref.at[slot, pl.ds(begin + which * (length // 2), length // 2), :]

    return part


def columns_part(ref, begin, length):
    def part(slot, which):
        width = ref.shape[-1]
        if which is None:
            return ref.at[slot, pl.ds(begin, length), :]
        return ref.at[slot, pl.ds(begin, length), pl.ds(which * (width // 2), width // 2)]

    return part


def mixer_kernel(
    tok,
    wx,
    wz,
    cw,
    cb,
    sw,
    ss,
    sg,
    wo,
    out,
    tg,
    gx,
    gz,
    go,
    acc_x,
    acc_z,
    xb,
    halo,
    ext,
    mw,
    keep,
    cum,
    read,
    pj,
    sb,
    st,
    part,
    pair,
    summed,
    landed,
    town,
    wx_send,
    wx_recv,
    wz_send,
    wz_recv,
    wo_send,
    wo_recv,
    tok_send,
    tok_recv,
    core_send,
    core_recv,
    halo_send,
    halo_recv,
    pj_send,
    pj_recv,
    st_send,
    st_recv,
    pair_send,
    pair_recv,
    sum_send,
    sum_recv,
):
    c, e = lax.axis_index("ctx"), lax.axis_index("exp")
    z, core = e // 2, lax.rem(e, 2)
    partner = z * 2 + 1 - core
    rows, inner = acc_x.shape

    gx[c] = wx[...]
    gz[c] = wz[...]
    go[c] = wo[...]
    tg[e] = tok[...]

    greet(True, True)

    weights = (
        PlaneGather(rows_part(gx, 0, gx.shape[1]), True, wx_send, wx_recv),
        PlaneGather(rows_part(gz, 0, gz.shape[1]), False, wz_send, wz_recv),
    )
    half = go.shape[1] // 2
    outs = (
        PlaneGather(rows_part(go, 0, half), True, wo_send.at[0], wo_recv.at[0]),
        PlaneGather(rows_part(go, half, half), False, wo_send.at[1], wo_recv.at[1]),
    )
    first_sends(weights)

    def tok_copy(d, slot):
        target = lax.rem(z + d, DEPTH) * 2 + core
        return remote(tg.at[slot], tg.at[slot], tok_send.at[d], tok_recv.at[d], (c, target))

    def core_copy(d, slot):
        return remote(tg.at[slot], tg.at[slot], core_send.at[d], core_recv.at[d], (c, partner))

    def from_z(d, k):
        return lax.rem(z - d + DEPTH, DEPTH) * 2 + k

    core_copy(0, e).start()

    @pl.loop(1, DEPTH)
    def _(d):
        tok_copy(d, e).start()

    first_hop(weights)

    @pl.loop(1, DEPTH)
    def _(d):
        tok_copy(d, from_z(d, core)).wait_recv()
        core_copy(d, from_z(d, core)).start()

    @pl.loop(0, DEPTH)
    def _(d):
        core_copy(d, from_z(d, 1 - core)).wait_recv()

    acc_x[...] = jnp.zeros_like(acc_x)
    acc_z[...] = jnp.zeros_like(acc_z)

    def multiply(acc, gathered, slot_of):
        @pl.loop(0, SIDE)
        def _(i):
            slot = slot_of(i)
            acc[...] += jnp.dot(tg[slot], gathered[slot], preferred_element_type=f32)

    first_axis_done(weights)
    view_x, view_z = weights[0].view, weights[1].view
    multiply(acc_x, gx, lambda i: view_x.at(i, 0))
    multiply(acc_z, gz, lambda i: view_z.at(i, 0))

    own_rows = out.shape[0]
    picked = lax.broadcasted_iota(jnp.int32, (own_rows, rows), 1) == (
        lax.broadcasted_iota(jnp.int32, (own_rows, rows), 0) + e * own_rows
    )
    picker = picked.astype(f32).astype(bf16)
    width = tg.shape[2]

    @pl.loop(0, EXPS)
    def _(j):
        town[j] = jnp.dot(picker, tg[j], preferred_element_type=f32)

    second_hop(weights)
    for step in (-1, 1):
        multiply(acc_x, gx, lambda i: view_x.at(i, step))
        multiply(acc_z, gz, lambda i: view_z.at(i, step))
    second_axis_done(weights)
    first_sends(outs)
    multiply(acc_x, gx, lambda i: view_x.at(i, 2))
    multiply(acc_z, gz, lambda i: view_z.at(i, 2))

    xb[...] = acc_x[...].astype(bf16)
    held = halo.shape[0]

    def halo_copy():
        return remote(
            xb.at[pl.ds(rows - held, held), :],
            halo,
            halo_send,
            halo_recv,
            (lax.rem(c + 1, PLANE), e),
        )

    @pl.when(c < PLANE - 1)
    def _():
        halo_copy().start()

    ext[pl.ds(held, rows), :] = xb[...].astype(f32)
    keep[...] = jnp.exp(-ss[...])

    @pl.when(c == 0)
    def _():
        halo[...] = jnp.zeros_like(halo)

    @pl.when(c > 0)
    def _():
        halo_copy().wait_recv()

    ext[pl.ds(0, held), :] = halo[...].astype(f32)
    filtered = jnp.broadcast_to(cb[...], (rows, inner))
    for offset in range(CONV):
        begin = held - (CONV - 1) + offset
        filtered = filtered + cw[pl.ds(offset, 1), :] * ext[pl.ds(begin, rows), :]
    mixer_in = (filtered / (1.0 + jnp.exp(-filtered))).astype(bf16)
    mw[...] = mixer_in.astype(f32)

    pj[e] = lax.dot_general(
        sw[...], mixer_in, (((0,), (1,)), ((), ())), preferred_element_type=f32
    )

    def pj_copy(d, slot):
        target = lax.rem(e + d, EXPS)
        return remote(pj.at[slot], pj.at[slot], pj_send.at[d], pj_recv.at[d], (c, target))

    @pl.loop(1, EXPS)
    def _(d):
        pj_copy(d, e).start()

    first_hop(outs)

    @pl.loop(1, EXPS)
    def _(d):
        pj_copy(d, lax.rem(e - d + EXPS, EXPS)).wait_recv()

    projected = pj[0]
    for j in range(1, EXPS):
        projected = projected + pj[j]
    chunks = rows // CHUNK
    for j in range(chunks):
        sb[j, :, pl.ds(0, CHUNK)] = projected[:, j * CHUNK : (j + 1) * CHUNK]

    def advance(j, carry):
        state, decay = carry
        vectors = sb[j]
        first = pl.multiple_of(j * CHUNK, CHUNK)
        keeps, inputs = keep[pl.ds(first, CHUNK), :], mw[pl.ds(first, CHUNK), :]
        for i in range(CHUNK):
            kept = keeps[i : i + 1, :]
            state = kept * state + inputs[i : i + 1, :] * vectors[:STATE, i : i + 1]
            decay = decay * kept
            read[pl.ds(first + i, 1), :] = jnp.sum(
                vectors[STATE:, i : i + 1] * state, axis=0, keepdims=True
            )
            cum[pl.ds(first + i, 1), :] = decay
        return state, decay

    state, decay = lax.fori_loop(
        0, chunks, advance, (jnp.zeros((STATE, inner), f32), jnp.ones((1, inner), f32))
    )

    st[c, pl.ds(0, STATE), :] = state
    st[c, pl.ds(STATE, 8), :] = jnp.broadcast_to(decay, (8, inner))

    def st_copy(d, slot, target):
        return remote(st.at[slot], st.at[slot], st_send.at[d], st_recv.at[d], (target, e))

    @pl.loop(1, PLANE - c)
    def _(d):
        st_copy(d, c, lax.rem(c + d, PLANE)).start()

    first_axis_done(outs)

    def enter(source, entering):
        st_copy(c - source, source, lax.rem(source + 1, PLANE)).wait_recv()
        return st[source, pl.ds(STATE, 1), :] * entering + st[source, pl.ds(0, STATE), :]

    entering = lax.fori_loop(0, c, enter, jnp.zeros((STATE, inner), f32))
    carried = cum[...] * lax.dot_general(
        projected[STATE:, :],
        entering,
        (((0,), (0,)), ((), ())),
        preferred_element_type=f32,
        precision=precise,
    )
    gate = acc_z[...].astype(bf16).astype(f32)
    mixed = (read[...] + carried + sg[...] * mw[...]) * (gate / (1.0 + jnp.exp(-gate)))
    xb_out = mixed.astype(bf16)
    second_hop(outs)
    second_axis_done(outs)

    columns = go.shape[2]

    @pl.loop(0, PLANE)
    def _(j):
        block = jnp.dot(xb_out, go[j], preferred_element_type=f32)
        at = pl.ds(pl.multiple_of(j * columns, columns), columns)
        for i in range(EXPS):
            part[i % 2, i // 2, :, at] = block[i * own_rows : (i + 1) * own_rows].astype(bf16)

    pair_copy = remote(part.at[1 - core], pair, pair_send, pair_recv, (c, partner))
    pair_copy.start()
    pair_copy.wait_recv()

    def sum_copy(d, mine, theirs, target):
        return remote(
            summed.at[mine], landed.at[theirs], sum_send.at[d], sum_recv.at[d], (c, target)
        )

    @pl.loop(1, DEPTH)
    def _(d):
        there = lax.rem(z + d, DEPTH)
        summed[there] = (part[core, there].astype(f32) + pair[there].astype(f32)).astype(bf16)
        sum_copy(d, there, z, there * 2 + core).start()

    for j in range(EXPS):
        out[:, pl.ds(j * width, width)] = town[j].astype(bf16)
    own = part[core, z].astype(f32) + pair[z].astype(f32)

    def collect(d, total):
        source = lax.rem(z - d + DEPTH, DEPTH)
        sum_copy(d, source, source, source * 2 + core).wait_recv()
        return total + landed[source].astype(f32)

    total = lax.fori_loop(1, DEPTH, collect, own)
    out[...] = (out[...].astype(f32) + total).astype(bf16)

    for g in weights + outs:
        g.finish()
    core_copy(0, e).wait_send()

    @pl.loop(1, DEPTH)
    def _(d):
        tok_copy(d, e).wait_send()
        core_copy(d, from_z(d, core)).wait_send()
        there = lax.rem(z + d, DEPTH)
        sum_copy(d, there, z, there * 2 + core).wait_send()

    @pl.when(c < PLANE - 1)
    def _():
        halo_copy().wait_send()

    @pl.loop(1, EXPS)
    def _(d):
        pj_copy(d, e).wait_send()

    @pl.loop(1, PLANE - c)
    def _(d):
        st_copy(d, c, lax.rem(c + d, PLANE)).wait_send()

    pair_copy.wait_send()


def mixer(tokens, wx, wz, cw, cb, sw, ss, sg, wo):
    rows, width = tokens.shape
    inner = wx.shape[1]
    model = width * EXPS
    own = rows // EXPS
    dma = pltpu.SemaphoreType.DMA
    vmem = pl.BlockSpec(memory_space=pltpu.VMEM)
    return pl.pallas_call(
        mixer_kernel,
        out_shape=jax.ShapeDtypeStruct((own, model), bf16),
        in_specs=[vmem] * 9,
        out_specs=vmem,
        scratch_shapes=[
            pltpu.VMEM((EXPS, rows, width), bf16),
            pltpu.VMEM((PLANE, *wx.shape), bf16),
            pltpu.VMEM((PLANE, *wz.shape), bf16),
            pltpu.VMEM((PLANE, *wo.shape), bf16),
            pltpu.VMEM((rows, inner), f32),
            pltpu.VMEM((rows, inner), f32),
            pltpu.VMEM((rows, inner), bf16),
            pltpu.VMEM((16, inner), bf16),
            pltpu.VMEM((rows + 16, inner), f32),
            pltpu.VMEM((rows, inner), f32),
            pltpu.VMEM((rows, inner), f32),
            pltpu.VMEM((rows, inner), f32),
            pltpu.VMEM((rows, inner), f32),
            pltpu.VMEM((EXPS, 2 * STATE, rows), f32),
            pltpu.VMEM((rows // CHUNK, 2 * STATE, 128), f32),
            pltpu.VMEM((PLANE, STATE + 8, inner), f32),
            pltpu.VMEM((2, DEPTH, own, model), bf16),
            pltpu.VMEM((DEPTH, own, model), bf16),
            pltpu.VMEM((DEPTH, own, model), bf16),
            pltpu.VMEM((DEPTH, own, model), bf16),
            pltpu.VMEM((EXPS, own, width), f32),
            dma((20,)),
            dma((20,)),
            dma((20,)),
            dma((20,)),
            dma((2, 20)),
            dma((2, 20)),
            dma((DEPTH,)),
            dma((DEPTH,)),
            dma((DEPTH,)),
            dma((DEPTH,)),
            dma,
            dma,
            dma((EXPS,)),
            dma((EXPS,)),
            dma((PLANE,)),
            dma((PLANE,)),
            dma,
            dma,
            dma((DEPTH,)),
            dma((DEPTH,)),
        ],
        compiler_params=pltpu.CompilerParams(
            collective_id=0, has_side_effects=True, vmem_limit_bytes=48 << 20
        ),
        name="mixer",
    )(tokens, wx, wz, cw, cb.reshape(1, -1), sw, ss, sg.reshape(1, -1), wo)


class PlaneReduce:
    ORDER = (2, -1, 1, 0)

    def __init__(self, part, late, x_first, send, recv):
        self.view, self.part, self.late = PlaneView(x_first), part, late
        self.send, self.recv = send, recv

    def place(self, k, step):
        if k < 16:
            return self.view.at(self.ORDER[k // 4], step)
        return self.view.at(step, 0)

    def copy(self, k):
        kind = k % 4
        step, which, to = ((2, 0, 1), (2, 1, -1), (1, None, 1), (-1, None, -1))[kind]
        target = self.view.at(0, to) if k < 16 else self.view.at(to, 0)
        return remote(
            self.part(self.place(k, step), which),
            self.late(k, which),
            self.send.at[k],
            self.recv.at[k],
            (target, self.view.e),
        )

    def add(self, k, step, which):
        self.copy(k).wait_recv()
        mine = self.part(self.place(k, step), which)
        mine[...] = (mine[...].astype(f32) + self.late(k, which)[...].astype(f32)).astype(bf16)

    def far(self, j):
        self.copy(4 * j).start()
        self.copy(4 * j + 1).start()

    def near(self, j):
        self.add(4 * j, 1, 0)
        self.copy(4 * j + 2).start()
        self.add(4 * j + 1, -1, 1)
        self.copy(4 * j + 3).start()

    def close(self, j):
        self.add(4 * j + 2, 0, None)
        self.add(4 * j + 3, 0, None)

    def finish(self):
        for k in range(20):
            self.copy(k).wait_send()


def expert_kernel(
    arrived,
    wg_hbm,
    wu_hbm,
    wd_hbm,
    out,
    wg,
    wu,
    wd,
    rows_in,
    acc_g,
    acc_u,
    sums,
    late,
    load_sem,
    ag_send,
    ag_recv,
    rs_send,
    rs_recv,
):
    c = lax.axis_index("ctx")
    loads = [
        pltpu.make_async_copy(src, dst, load_sem.at[i])
        for i, (src, dst) in enumerate(((wg_hbm, wg), (wu_hbm, wu), (wd_hbm, wd)))
    ]
    for load in loads:
        load.start()
    rows_in[c] = arrived[...]
    greet(True, False)
    slots, model = arrived.shape
    half = slots // 2
    gathers = (
        PlaneGather(columns_part(rows_in, 0, half), True, ag_send.at[0], ag_recv.at[0]),
        PlaneGather(columns_part(rows_in, half, half), False, ag_send.at[1], ag_recv.at[1]),
    )
    first_sends(gathers)
    first_hop(gathers)
    first_axis_done(gathers)
    second_hop(gathers)
    second_axis_done(gathers)
    for load in loads:
        load.wait()

    units = wg.shape[0]
    many = PLANE * slots
    step = 512
    acc_g[...] = jnp.zeros_like(acc_g)
    acc_u[...] = jnp.zeros_like(acc_u)

    @pl.loop(0, model // step)
    def _(k):
        at = pl.ds(pl.multiple_of(k * step, step), step)
        block = rows_in[:, :, at].reshape(many, step)
        turned = (((1,), (1,)), ((), ()))
        acc_g[...] += lax.dot_general(block, wg[:, at], turned, preferred_element_type=f32)
        acc_u[...] += lax.dot_general(block, wu[:, at], turned, preferred_element_type=f32)

    gate = acc_g[...]
    hidden = ((gate / (1.0 + jnp.exp(-gate))) * acc_u[...]).astype(bf16)

    @pl.loop(0, model // step)
    def _(k):
        at = pl.ds(pl.multiple_of(k * step, step), step)
        block = jnp.dot(hidden, wd[:, at], preferred_element_type=f32)
        sums[:, :, at] = block.astype(bf16).reshape(PLANE, slots, step)

    def landing(i):
        def at(k, which):
            if which is None:
                return late.at[i, k]
            return late.at[i, k, :, pl.ds(which * (model // 2), model // 2)]

        return at

    reduces = (
        PlaneReduce(columns_part(sums, 0, half), landing(0), True, rs_send.at[0], rs_recv.at[0]),
        PlaneReduce(columns_part(sums, half, half), landing(1), False, rs_send.at[1], rs_recv.at[1]),
    )
    for j in range(4):
        for r in reduces:
            r.far(j)
    for j in range(4):
        for r in reduces:
            r.near(j)
    for j in range(4):
        for r in reduces:
            r.close(j)
            if j == 0:
                r.far(4)
    for r in reduces:
        r.near(4)
    for r in reduces:
        r.close(4)
    out[...] = sums[c]
    for g in gathers:
        g.finish()
    for r in reduces:
        r.finish()


def experts_of(arrived, wg, wu, wd):
    slots, model = arrived.shape
    units = wg.shape[0]
    dma = pltpu.SemaphoreType.DMA
    vmem = pl.BlockSpec(memory_space=pltpu.VMEM)
    anywhere = pl.BlockSpec(memory_space=pl.ANY)
    return pl.pallas_call(
        expert_kernel,
        out_shape=jax.ShapeDtypeStruct((slots, model), bf16),
        in_specs=[vmem, anywhere, anywhere, anywhere],
        out_specs=vmem,
        scratch_shapes=[
            pltpu.VMEM((units, model), bf16),
            pltpu.VMEM((units, model), bf16),
            pltpu.VMEM((units, model), bf16),
            pltpu.VMEM((PLANE, slots, model), bf16),
            pltpu.VMEM((PLANE * slots, units), f32),
            pltpu.VMEM((PLANE * slots, units), f32),
            pltpu.VMEM((PLANE, slots, model), bf16),
            pltpu.VMEM((2, 20, slots // 2, model), bf16),
            dma((3,)),
            dma((2, 20)),
            dma((2, 20)),
            dma((2, 20)),
            dma((2, 20)),
        ],
        compiler_params=pltpu.CompilerParams(
            collective_id=1, has_side_effects=True, vmem_limit_bytes=56 << 20
        ),
        name="experts",
    )(arrived, wg, wu, wd)


def exchange_kernel(given, taken, own_sem, send, recv):
    c, e = lax.axis_index("ctx"), lax.axis_index("exp")
    own = pltpu.make_async_copy(given.at[e], taken.at[e], own_sem)
    own.start()
    greet(False, True)

    def copy(d, mine, theirs, target):
        return remote(given.at[mine], taken.at[theirs], send.at[d], recv.at[d], (c, target))

    @pl.loop(1, EXPS)
    def _(d):
        there = lax.rem(e + d, EXPS)
        copy(d, there, e, there).start()

    own.wait()

    @pl.loop(1, EXPS)
    def _(d):
        source = lax.rem(e - d + EXPS, EXPS)
        copy(d, source, source, source).wait_recv()

    @pl.loop(1, EXPS)
    def _(d):
        there = lax.rem(e + d, EXPS)
        copy(d, there, e, there).wait_send()


def exchange(blocks, collective_id):
    dma = pltpu.SemaphoreType.DMA
    vmem = pl.BlockSpec(memory_space=pltpu.VMEM)
    return pl.pallas_call(
        exchange_kernel,
        out_shape=jax.ShapeDtypeStruct(blocks.shape, blocks.dtype),
        in_specs=[vmem],
        out_specs=vmem,
        scratch_shapes=[dma, dma((EXPS,)), dma((EXPS,))],
        compiler_params=pltpu.CompilerParams(collective_id=collective_id, has_side_effects=True),
        name=f"exchange_{collective_id}",
    )(blocks)


def local(
    tokens,
    input_weight,
    gate_weight,
    conv_weight,
    conv_bias,
    state_weight,
    step_size,
    skip_gain,
    output_weight,
    norm_gain,
    router_weight,
    expert_gate,
    expert_up,
    expert_down,
    expert_ids,
):
    residual = mixer(
        tokens,
        input_weight,
        gate_weight,
        conv_weight,
        conv_bias,
        state_weight,
        step_size,
        skip_gain,
        output_weight,
    )
    row_count = expert_ids.shape[0]
    stream = residual.astype(f32)
    normed = (
        stream
        * lax.rsqrt(jnp.mean(stream * stream, -1, keepdims=True) + 1e-05)
        * norm_gain[None, :]
    ).astype(bf16)
    logits = jnp.dot(normed, router_weight, preferred_element_type=f32)
    experts = router_weight.shape[1]
    expert_range = jnp.arange(experts, dtype=jnp.int32)
    chosen = expert_ids[:, :, None] == expert_range[None, None, :]
    selected_entry = jnp.sum(jnp.where(chosen, logits[:, None, :], 0.0), -1)
    shares = jax.nn.sigmoid(selected_entry - selected_entry[:, ::-1])
    flat_hits = chosen.reshape(row_count * TOP, experts).astype(f32)
    earlier_hits = jnp.dot(
        jnp.tril(jnp.ones((row_count * TOP, row_count * TOP), f32), -1),
        flat_hits,
        precision=precise,
    )
    slot_index = jnp.sum(earlier_hits * flat_hits, -1).astype(jnp.int32)
    target = expert_ids.reshape(-1) * CAP + slot_index
    placed = target[:, None] == jnp.arange(experts * CAP, dtype=jnp.int32)[None, :]
    placed = placed.reshape(row_count, TOP, experts * CAP)
    selector = jnp.any(placed, 1).astype(bf16)
    outgoing = lax.dot_general(
        selector, normed, (((0,), (0,)), ((), ())), preferred_element_type=f32
    ).astype(bf16)
    outgoing = outgoing.reshape(experts, CAP, -1)
    arrived = exchange(outgoing, 2).reshape(experts * CAP, -1)
    finished = experts_of(arrived, expert_gate[0], expert_up[0], expert_down[0])
    returned = exchange(finished.reshape(experts, CAP, -1), 3)
    returned = returned.reshape(experts * CAP, -1).astype(f32)
    combine = jnp.sum(jnp.where(placed, shares[:, :, None], 0.0), 1)
    moe_out = jnp.dot(combine, returned, precision=precise)
    return (stream + moe_out).astype(bf16)


def solution(mesh):
    in_specs = (
        P("ctx", "exp"),
        P("ctx", "exp"),
        P("ctx", "exp"),
        P(None, "exp"),
        P("exp"),
        P("exp", None),
        P("ctx", "exp"),
        P("exp"),
        P("exp", "ctx"),
        P(),
        P(),
        P("exp", "ctx", None),
        P("exp", "ctx", None),
        P("exp", "ctx", None),
        P(("ctx", "exp"), None),
    )
    out_specs = P(("ctx", "exp"), None)
    return jax.shard_map(local, mesh=mesh, in_specs=in_specs, out_specs=out_specs, check_vma=False)
```

```python
import functools

import jax
import jax.numpy as jnp
from jax import lax
from jax.experimental import pallas as pl
from jax.experimental.pallas import tpu as pltpu
from jax.sharding import PartitionSpec as P

STATE = 16
CONV = 4
TOP = 2
CAP = 2
SIDE = 4
PLANE = SIDE * SIDE
DEPTH = 8
EXPS = 2 * DEPTH
CHUNK = 8

precise = lax.Precision.HIGHEST
f32 = jnp.float32
bf16 = jnp.bfloat16
MESH = pl.DeviceIdType.MESH


def remote(src, dst, send_sem, recv_sem, device):
    return pltpu.make_async_remote_copy(
        src_ref=src,
        dst_ref=dst,
        send_sem=send_sem,
        recv_sem=recv_sem,
        device_id=device,
        device_id_type=MESH,
    )


def greeting(*groups):
    barrier = pltpu.get_barrier_semaphore()
    for count, device_of in groups:

        @pl.loop(1, count)
        def _(d):
            pl.semaphore_signal(barrier, inc=1, device_id=device_of(d), device_id_type=MESH)

    return lambda: pl.semaphore_wait(barrier, sum(count - 1 for count, _ in groups))


class PlaneView:
    def __init__(self, x_first):
        c, self.e = lax.axis_index("ctx"), lax.axis_index("exp")
        y, x = c // SIDE, lax.rem(c, SIDE)
        self.x_first = x_first
        self.f, self.s = (x, y) if x_first else (y, x)

    def at(self, df, ds):
        f, s = lax.rem(self.f + df + SIDE, SIDE), lax.rem(self.s + ds + SIDE, SIDE)
        return s * SIDE + f if self.x_first else f * SIDE + s


class PlaneGather:
    ORDER = (0, -1, 1, 2)

    def __init__(self, part, x_first, send, recv):
        self.view, self.part, self.send, self.recv = PlaneView(x_first), part, send, recv

    def copy(self, k, slot, which, target):
        block = self.part(slot, which)
        return remote(block, block, self.send.at[k], self.recv.at[k], (target, self.view.e))

    def sent(self, k):
        at = self.view.at
        if k < 4:
            slot, which = ((0, None), (0, None), (-1, 0), (1, 1))[k]
            return self.copy(k, at(slot, 0), which, at(1 if k % 2 == 0 else -1, 0))
        df, kind = self.ORDER[(k - 4) // 4], (k - 4) % 4
        slot, which = ((0, None), (0, None), (-1, 0), (1, 1))[kind]
        return self.copy(k, at(df, slot), which, at(0, 1 if kind % 2 == 0 else -1))

    def arrived(self, k):
        at = self.view.at
        if k < 4:
            slot, which = ((-1, None), (1, None), (2, 0), (2, 1))[k]
            return self.copy(k, at(slot, 0), which, at(0, 0))
        df, kind = self.ORDER[(k - 4) // 4], (k - 4) % 4
        slot, which = ((-1, None), (1, None), (2, 0), (2, 1))[kind]
        return self.copy(k, at(df, slot), which, at(0, 0))

    def start(self, *ks):
        for k in ks:
            self.sent(k).start()

    def await_(self, *ks):
        for k in ks:
            self.arrived(k).wait_recv()

    def finish(self, ks=range(20)):
        for k in ks:
            self.sent(k).wait_send()


def first_sends(gathers):
    for g in gathers:
        g.start(0, 1)
    for g in gathers:
        g.start(4, 5)


def first_hop(gathers):
    for g in gathers:
        g.await_(0)
        g.start(2, 8, 9)
        g.await_(1)
        g.start(3, 12, 13)


def first_axis_done(gathers):
    for g in gathers:
        g.await_(2, 3)
        g.start(16, 17)


def second_hop_of(gathers, j):
    for g in gathers:
        g.await_(4 + 4 * j)
        g.start(6 + 4 * j)
        g.await_(5 + 4 * j)
        g.start(7 + 4 * j)


def second_hop(gathers):
    for j in range(SIDE):
        second_hop_of(gathers, j)


def second_axis_done(gathers):
    for j in range(4):
        for g in gathers:
            g.await_(6 + 4 * j, 7 + 4 * j)


def rows_part(ref, begin, length):
    def part(slot, which):
        if which is None:
            return ref.at[slot, pl.ds(begin, length), :]
        return ref.at[slot, pl.ds(begin + which * (length // 2), length // 2), :]

    return part


def mixer_kernel(
    tok,
    wx,
    wz,
    cw_hbm,
    cb_hbm,
    sw_hbm,
    ss,
    sg_hbm,
    wo,
    out,
    tg,
    gw,
    go,
    cw,
    cb,
    sw,
    sg,
    steps,
    acc,
    gate,
    ext,
    tail,
    halo,
    mw,
    keep,
    cum,
    read,
    q0,
    q1,
    q2,
    q3,
    sb,
    st,
    mg,
    ml,
    part,
    pair,
    summed,
    landed,
    leave,
    fin,
    town,
    load_sem,
    x_send,
    x_recv,
    z_send,
    z_recv,
    core_send,
    core_recv,
    gw_send,
    gw_recv,
    go_send,
    go_recv,
    halo_send,
    halo_recv,
    q_send,
    q_recv,
    st_send,
    st_recv,
    mg_send,
    mg_recv,
    pair_send,
    pair_recv,
    sum_send,
    sum_recv,
    fin_send,
    fin_recv,
):
    c, e = lax.axis_index("ctx"), lax.axis_index("exp")
    y, x = c // SIDE, lax.rem(c, SIDE)
    z, core = e // 2, lax.rem(e, 2)
    partner = z * 2 + 1 - core
    rows, width = tok.shape
    lanes = wx.shape[1] // SIDE
    own_rows = out.shape[0]

    def around(value, size):
        return lax.rem(value + size, size)

    def in_row(index):
        return y * SIDE + index // 2, z * 2 + lax.rem(index, 2)

    def along_z(d):
        return c, around(z + d, DEPTH) * 2 + core

    def along_y(d):
        return around(y + d, SIDE) * SIDE + x, e

    spot = x * 2 + core
    spots = 2 * SIDE
    meet = greeting(
        (spots, lambda d: in_row(around(spot + d, spots))), (DEPTH, along_z), (SIDE, along_y)
    )

    def columns(block):
        return pl.ds(pl.multiple_of(block * lanes, lanes), lanes)

    mine = columns(x)
    loads = [
        pltpu.make_async_copy(source, place, load_sem.at[i])
        for i, (source, place) in enumerate(
            (
                (tok, tg.at[e, x]),
                (wx.at[:, mine], gw.at[c, :, pl.ds(0, lanes)]),
                (wz.at[:, mine], gw.at[c, :, pl.ds(lanes, lanes)]),
                (ss.at[:, mine], steps.at[x]),
                (cw_hbm.at[:, mine], cw),
                (cb_hbm.at[:, mine], cb),
                (sw_hbm.at[:, mine], sw),
                (sg_hbm.at[:, mine], sg),
                (wo, go.at[y]),
            )
        )
    ]
    for load in loads:
        load.start()
    meet()

    def x_copy(i, d, source, to):
        slot = y * SIDE + source
        src, dst = (
            (tok, tg.at[e, source]),
            (wx.at[:, columns(to)], gw.at[slot, :, pl.ds(0, lanes)]),
            (wz.at[:, columns(to)], gw.at[slot, :, pl.ds(lanes, lanes)]),
            (ss.at[:, columns(to)], steps.at[source]),
        )[i]
        return remote(src, dst, x_send.at[i, d], x_recv.at[i, d], (y * SIDE + to, e))

    for i in range(4):
        for d in (1, 3, 2):
            x_copy(i, d, x, around(x + d, SIDE)).start()

    def z_part(zz, s, which):
        slot = around(zz, DEPTH) * 2 + core
        if which is None:
            return tg.at[slot, s]
        return tg.at[slot, s, pl.ds(which * (rows // 2), rows // 2), :]

    def z_copy(way, hop, s, sender):
        block = sender - (hop - 1) if way == 0 else sender + (hop - 1)
        ref = z_part(block + DEPTH, s, None if hop < 4 else way)
        to = around(sender + (1 if way == 0 else -1) + DEPTH, DEPTH) * 2 + core
        return remote(ref, ref, z_send.at[way, hop - 1, s], z_recv.at[way, hop - 1, s], (c, to))

    def z_sent(way, hop, s):
        return z_copy(way, hop, s, z)

    def z_arrived(way, hop, s):
        return z_copy(way, hop, s, z - 1 if way == 0 else z + 1)

    def core_copy(zz, k):
        ref = tg.at[zz * 2 + k]
        return remote(ref, ref, core_send.at[zz], core_recv.at[zz], (c, partner))

    order = [around(x + d, SIDE) for d in PlaneGather.ORDER]
    weights = PlaneGather(
        rows_part(gw, 0, gw.shape[1]), True, gw_send, gw_recv
    )
    loads[0].wait()
    for way in range(2):
        z_sent(way, 1, x).start()
    loads[1].wait()
    loads[2].wait()
    weights.start(4, 5)
    for i, d in ((1, 1), (2, 3), (3, 2)):
        x_copy(0, d, order[i], x).wait_recv()
        for way in range(2):
            z_sent(way, 1, order[i]).start()
        x_copy(1, d, order[i], x).wait_recv()
        x_copy(2, d, order[i], x).wait_recv()
        weights.start(4 + 4 * i, 5 + 4 * i)
    core_copy(z, core).start()

    def z_hop(hop):
        for s in order:
            for way in range(2):
                z_arrived(way, hop, s).wait_recv()
                if hop < 4:
                    z_sent(way, hop + 1, s).start()
        core_copy(around(z - hop, DEPTH), core).start()
        if hop < 4:
            core_copy(around(z + hop, DEPTH), core).start()

    second_hop_of((weights,), 0)
    z_hop(1)
    second_hop_of((weights,), 1)
    second_hop_of((weights,), 2)
    z_hop(2)
    second_hop_of((weights,), 3)
    z_hop(3)
    second_axis_done((weights,))
    outs = PlaneGather(
        lambda slot, which: go.at[slot // SIDE]
        if which is None
        else go.at[slot // SIDE, pl.ds(which * (go.shape[1] // 2), go.shape[1] // 2), :],
        False,
        go_send,
        go_recv,
    )
    for load in loads[3:]:
        load.wait()
    outs.start(0, 1)
    for d in (1, 2, 3):
        x_copy(3, d, around(x - d, SIDE), x).wait_recv()
    keep[...] = jnp.exp(-jnp.concatenate([steps[s] for s in range(SIDE)], axis=1))
    z_hop(4)

    @pl.loop(0, DEPTH)
    def _(zz):
        core_copy(zz, 1 - core).wait_recv()

    acc[...] = jnp.zeros_like(acc)
    many = SIDE * rows

    @pl.loop(0, EXPS)
    def _(j):
        acc[...] += jnp.dot(tg[j].reshape(many, width), gw[j], preferred_element_type=f32)

    held = halo.shape[0]
    tail[...] = acc[pl.ds(many - held, held), pl.ds(0, lanes)].astype(bf16)

    def halo_copy():
        return remote(tail, halo, halo_send, halo_recv, along_y(1))

    @pl.when(y < SIDE - 1)
    def _():
        halo_copy().start()

    for s in range(SIDE):
        at = pl.ds(s * lanes, lanes)
        here = pl.ds(s * rows, rows)
        ext[pl.ds(held, rows), at] = acc[here, pl.ds(0, lanes)].astype(bf16).astype(f32)
        gate[:, at] = acc[here, pl.ds(lanes, lanes)].astype(bf16).astype(f32)
        if s:
            ext[pl.ds(0, held), at] = ext[pl.ds(rows, held), pl.ds((s - 1) * lanes, lanes)]

    @pl.when(y == 0)
    def _():
        halo[...] = jnp.zeros_like(halo)

    @pl.when(y > 0)
    def _():
        halo_copy().wait_recv()

    ext[pl.ds(0, held), pl.ds(0, lanes)] = halo[...].astype(f32)

    def spread(values):
        return jnp.concatenate([values] * SIDE, axis=1)

    filtered = jnp.broadcast_to(spread(cb[...]), keep.shape)
    for offset in range(CONV):
        begin = held - (CONV - 1) + offset
        tap = spread(cw[pl.ds(offset, 1), :])
        filtered = filtered + tap * ext[pl.ds(begin, rows), :]
    mixer_in = (filtered / (1.0 + jnp.exp(-filtered))).astype(bf16)
    mw[...] = mixer_in.astype(f32)

    for s in range(SIDE):
        both = lax.dot_general(
            sw[...],
            mixer_in[:, s * lanes : (s + 1) * lanes],
            (((1,), (1,)), ((), ())),
            preferred_element_type=f32,
        )
        q0[2 * s] = both[:STATE]
        q0[2 * s + 1] = both[STATE:]

    def to_sum(d, source, there):
        return remote(
            q0.at[there], q1.at[source], q_send.at[0, d], q_recv.at[0, d], in_row(there)
        )

    def z_sum(d, source):
        return remote(q2.at[source], q2.at[source], q_send.at[1, d], q_recv.at[1, d], along_z(d))

    def to_share(d, source, there):
        return remote(
            q3.at[source], q3.at[source], q_send.at[2, d], q_recv.at[2, d], in_row(there)
        )

    @pl.loop(1, spots)
    def _(d):
        to_sum(d, spot, around(spot + d, spots)).start()

    q1[spot] = q0[spot]
    outs.await_(0)
    outs.start(2)
    outs.await_(1)
    outs.start(3)

    picked = lax.broadcasted_iota(jnp.int32, (own_rows, rows), 1) == (
        lax.broadcasted_iota(jnp.int32, (own_rows, rows), 0) + e * own_rows
    )
    picker = picked.astype(f32).astype(bf16)

    @pl.loop(0, EXPS)
    def _(j):
        town[j] = jnp.dot(picker, tg[j, x], preferred_element_type=f32)

    @pl.loop(1, spots)
    def _(d):
        to_sum(d, around(spot - d, spots), spot).wait_recv()

    total = q1[0]
    for j in range(1, spots):
        total = total + q1[j]
    q2[z] = total

    @pl.loop(1, DEPTH)
    def _(d):
        z_sum(d, z).start()

    @pl.loop(1, DEPTH)
    def _(d):
        z_sum(d, around(z - d, DEPTH)).wait_recv()

    total = q2[0]
    for j in range(1, DEPTH):
        total = total + q2[j]
    q3[spot] = total

    @pl.loop(1, spots)
    def _(d):
        to_share(d, spot, around(spot + d, spots)).start()

    @pl.loop(1, spots)
    def _(d):
        to_share(d, around(spot - d, spots), spot).wait_recv()

    chunks = rows // CHUNK
    for k in range(2):
        for s in range(SIDE):
            vectors = q3[2 * s + k]
            for j in range(chunks):
                sb[j, pl.ds(k * STATE, STATE), pl.ds(s * CHUNK, CHUNK)] = vectors[
                    :, j * CHUNK : (j + 1) * CHUNK
                ]

    def advance(j, carry):
        state, decay = carry
        vectors = sb[j]
        first = pl.multiple_of(j * CHUNK, CHUNK)
        keeps, inputs = keep[pl.ds(first, CHUNK), :], mw[pl.ds(first, CHUNK), :]

        def vector(begin, i):
            picks = [
                jnp.broadcast_to(
                    vectors[begin : begin + STATE, s * CHUNK + i : s * CHUNK + i + 1],
                    (STATE, lanes),
                )
                for s in range(SIDE)
            ]
            return jnp.concatenate(picks, axis=1)

        for i in range(CHUNK):
            kept = keeps[i : i + 1, :]
            state = kept * state + inputs[i : i + 1, :] * vector(0, i)
            decay = decay * kept
            read[pl.ds(first + i, 1), :] = jnp.sum(
                vector(STATE, i) * state, axis=0, keepdims=True
            )
            cum[pl.ds(first + i, 1), :] = decay
        return state, decay

    wide = SIDE * lanes
    state, decay = lax.fori_loop(
        0, chunks, advance, (jnp.zeros((STATE, wide), f32), jnp.ones((1, wide), f32))
    )

    ends = [state[:, s * lanes : (s + 1) * lanes] for s in range(SIDE)]
    keeps = [decay[:, s * lanes : (s + 1) * lanes] for s in range(SIDE)]
    row_end, row_keep = ends[0], keeps[0]
    for s in range(1, SIDE):
        row_end, row_keep = keeps[s] * row_end + ends[s], keeps[s] * row_keep
    st[y, pl.ds(0, STATE), :] = row_end
    st[y, pl.ds(STATE, 8), :] = jnp.broadcast_to(row_keep, (8, lanes))

    def st_copy(d, slot):
        return remote(st.at[slot], st.at[slot], st_send.at[d], st_recv.at[d], along_y(d))

    @pl.loop(1, SIDE - y)
    def _(d):
        st_copy(d, y).start()

    gated = gate[...] / (1.0 + jnp.exp(-gate[...]))
    inside = read[...] + spread(sg[...]) * mw[...]

    def enter(source, entering):
        st_copy(y - source, source).wait_recv()
        return st[source, pl.ds(STATE, 1), :] * entering + st[source, pl.ds(0, STATE), :]

    entering = lax.fori_loop(0, y, enter, jnp.zeros((STATE, lanes), f32))
    carried = []
    for s in range(SIDE):
        carried.append(
            lax.dot_general(
                q3[2 * s + 1],
                entering,
                (((0,), (0,)), ((), ())),
                preferred_element_type=f32,
                precision=precise,
            )
        )
        entering = keeps[s] * entering + ends[s]
    mixed = (inside + cum[...] * jnp.concatenate(carried, axis=1)) * gated
    for s in range(SIDE):
        mg[x, s] = mixed[:, s * lanes : (s + 1) * lanes].astype(bf16)

    def mg_part(slot, which):
        at = lax.rem(slot, SIDE)
        return mg.at[at] if which is None else mg.at[at, pl.ds(which * 2, 2)]

    channels = PlaneGather(mg_part, True, mg_send, mg_recv)
    channels.start(0, 1)
    outs.await_(2, 3)
    channels.await_(0)
    channels.start(2)
    channels.await_(1)
    channels.start(3)
    channels.await_(2, 3)
    for s in range(SIDE):
        ml[:, pl.ds(s * lanes, lanes)] = mg[s].reshape(many, lanes)

    block_columns = go.shape[2]

    @pl.loop(0, SIDE)
    def _(j):
        block = jnp.dot(ml[...], go[j], preferred_element_type=f32)
        at = pl.ds(pl.multiple_of(j * block_columns, block_columns), block_columns)
        for i in range(EXPS):
            for s in range(SIDE):
                begin = s * rows + i * own_rows
                part[i % 2, i // 2, s, :, at] = block[begin : begin + own_rows].astype(bf16)

    pair_copy = remote(part.at[1 - core], pair, pair_send, pair_recv, (c, partner))
    pair_copy.start()
    pair_copy.wait_recv()

    def sum_copy(d, there, source):
        return remote(
            summed.at[there], landed.at[source], sum_send.at[d], sum_recv.at[d], along_z(d)
        )

    @pl.loop(1, DEPTH)
    def _(d):
        there = around(z + d, DEPTH)
        summed[there] = (part[core, there].astype(f32) + pair[there].astype(f32)).astype(bf16)
        sum_copy(d, there, z).start()

    def collect(d, total):
        source = around(z - d, DEPTH)
        sum_copy(d, z, source).wait_recv()
        return total + landed[source].astype(f32)

    total = lax.fori_loop(
        1, DEPTH, collect, part[core, z].astype(f32) + pair[z].astype(f32)
    )
    leave[...] = total.astype(bf16)

    def fin_copy(d, there, source):
        return remote(
            leave.at[there], fin.at[source], fin_send.at[d], fin_recv.at[d], (y * SIDE + there, e)
        )

    for d in (1, 3, 2):
        fin_copy(d, around(x + d, SIDE), x).start()
    fin[x] = leave[x]
    for d in (1, 3, 2):
        fin_copy(d, x, around(x - d, SIDE)).wait_recv()
    for i in range(SIDE):
        for s in range(SIDE):
            block = i * SIDE + s
            term = fin[s, :, pl.ds(i * block_columns, block_columns)].astype(f32)
            out[:, pl.ds(block * width, width)] = (town[block] + term).astype(bf16)

    for d in (1, 2, 3):
        for i in range(4):
            x_copy(i, d, x, around(x + d, SIDE)).wait_send()
        fin_copy(d, around(x + d, SIDE), x).wait_send()
    for s in order:
        for way in range(2):
            for hop in range(1, 5):
                z_sent(way, hop, s).wait_send()
    weights.finish(range(4, 20))
    outs.finish(range(4))
    channels.finish(range(4))

    @pl.loop(0, DEPTH)
    def _(zz):
        core_copy(zz, core).wait_send()

    @pl.when(y < SIDE - 1)
    def _():
        halo_copy().wait_send()

    @pl.loop(1, spots)
    def _(d):
        to_sum(d, spot, around(spot + d, spots)).wait_send()
        z_sum(d, z).wait_send()
        to_share(d, spot, around(spot + d, spots)).wait_send()
        sum_copy(d, around(z + d, DEPTH), z).wait_send()

    @pl.loop(1, SIDE - y)
    def _(d):
        st_copy(d, y).wait_send()

    pair_copy.wait_send()


def mixer(tokens, wx, wz, cw, cb, sw, ss, sg, wo):
    rows, width = tokens.shape
    depth, inner = wx.shape
    lanes = inner // SIDE
    model = width * EXPS
    own = rows // EXPS
    dma = pltpu.SemaphoreType.DMA
    vmem = pltpu.VMEM
    wide = vmem((rows, inner), f32)
    spread = (DEPTH, SIDE, own, model // SIDE)
    vectors = vmem((2 * SIDE, STATE, rows), f32)
    return pl.pallas_call(
        mixer_kernel,
        out_shape=jax.ShapeDtypeStruct((own, model), bf16),
        in_specs=[pl.BlockSpec(memory_space=pltpu.HBM)] * 9,
        out_specs=pl.BlockSpec(memory_space=pltpu.VMEM),
        scratch_shapes=[
            vmem((EXPS, SIDE, rows, width), bf16),
            vmem((PLANE, depth, 2 * lanes), bf16),
            vmem((SIDE, *wo.shape), bf16),
            vmem((CONV, lanes), f32),
            vmem((1, lanes), f32),
            vmem((2 * STATE, lanes), bf16),
            vmem((1, lanes), f32),
            vmem((SIDE, rows, lanes), f32),
            vmem((SIDE * rows, 2 * lanes), f32),
            wide,
            vmem((rows + 16, inner), f32),
            vmem((16, lanes), bf16),
            vmem((16, lanes), bf16),
            wide,
            wide,
            wide,
            wide,
            vectors,
            vectors,
            vmem((DEPTH, STATE, rows), f32),
            vectors,
            vmem((rows // CHUNK, 2 * STATE, 128), f32),
            vmem((SIDE, STATE + 8, lanes), f32),
            vmem((SIDE, SIDE, rows, lanes), bf16),
            vmem((SIDE * rows, inner), bf16),
            vmem((2, *spread), bf16),
            vmem(spread, bf16),
            vmem(spread, bf16),
            vmem(spread, bf16),
            vmem(spread[1:], bf16),
            vmem(spread[1:], bf16),
            vmem((EXPS, own, width), f32),
            dma((9,)),
            dma((4, SIDE)),
            dma((4, SIDE)),
            dma((2, 4, SIDE)),
            dma((2, 4, SIDE)),
            dma((DEPTH,)),
            dma((DEPTH,)),
            dma((20,)),
            dma((20,)),
            dma((4,)),
            dma((4,)),
            dma,
            dma,
            dma((3, DEPTH)),
            dma((3, DEPTH)),
            dma((SIDE,)),
            dma((SIDE,)),
            dma((4,)),
            dma((4,)),
            dma,
            dma,
            dma((DEPTH,)),
            dma((DEPTH,)),
            dma((SIDE,)),
            dma((SIDE,)),
        ],
        compiler_params=pltpu.CompilerParams(
            collective_id=0, has_side_effects=True, vmem_limit_bytes=62 << 20
        ),
        name="mixer",
    )(tokens, wx, wz, cw, cb.reshape(1, -1), sw.T, ss, sg.reshape(1, -1), wo)


class PlaneReduce:
    ORDER = (2, -1, 1, 0)

    def __init__(self, part, late, x_first, send, recv):
        self.view, self.part, self.late = PlaneView(x_first), part, late
        self.send, self.recv = send, recv

    def place(self, k, step):
        if k < 16:
            return self.view.at(self.ORDER[k // 4], step)
        return self.view.at(step, 0)

    def copy(self, k):
        kind = k % 4
        step, which, to = ((2, 0, 1), (2, 1, -1), (1, None, 1), (-1, None, -1))[kind]
        target = self.view.at(0, to) if k < 16 else self.view.at(to, 0)
        return remote(
            self.part(self.place(k, step), which),
            self.late(k, which),
            self.send.at[k],
            self.recv.at[k],
            (target, self.view.e),
        )

    def add(self, k, step, which):
        self.copy(k).wait_recv()
        mine = self.part(self.place(k, step), which)
        mine[...] = (mine[...].astype(f32) + self.late(k, which)[...].astype(f32)).astype(bf16)

    def far(self, j):
        self.copy(4 * j).start()
        self.copy(4 * j + 1).start()

    def near(self, j):
        self.add(4 * j, 1, 0)
        self.copy(4 * j + 2).start()
        self.add(4 * j + 1, -1, 1)
        self.copy(4 * j + 3).start()

    def close(self, j):
        self.add(4 * j + 2, 0, None)
        self.add(4 * j + 3, 0, None)

    def finish(self):
        for k in range(20):
            self.copy(k).wait_send()


def chunk_part(ref, row, rows, column, columns):
    def part(slot, which):
        if which is None:
            return ref.at[slot, pl.ds(row, rows), pl.ds(column, columns)]
        half = columns // 2
        return ref.at[slot, pl.ds(row, rows), pl.ds(column + which * half, half)]

    return part


def expert_kernel(
    normed,
    selector,
    combine,
    residual,
    wg_hbm,
    wu_hbm,
    wd_hbm,
    out,
    wg,
    wu,
    wd,
    give,
    take,
    back,
    ret,
    packed,
    rows_in,
    acc_g,
    acc_u,
    sums,
    late,
    load_sem,
    out_send,
    out_recv,
    back_send,
    back_recv,
    ag_send,
    ag_recv,
    rs_send,
    rs_recv,
):
    c, e = lax.axis_index("ctx"), lax.axis_index("exp")
    loads = [
        pltpu.make_async_copy(src, dst, load_sem.at[i])
        for i, (src, dst) in enumerate(((wg_hbm, wg), (wu_hbm, wu), (wd_hbm, wd)))
    ]
    for load in loads:
        load.start()
    meet = greeting(
        (PLANE, lambda d: (lax.rem(c + d, PLANE), e)), (EXPS, lambda d: (c, lax.rem(e + d, EXPS)))
    )
    slots, model = packed.shape
    units = wg.shape[0]
    turned = (((1,), (1,)), ((), ()))

    packed[...] = jnp.dot(selector[...], normed[...], preferred_element_type=f32)
    for j in range(EXPS):
        give[j] = packed[pl.ds(j * CAP, CAP), :].astype(bf16)
    take[e] = give[e]
    meet()

    def out_copy(there, source):
        return remote(
            give.at[there], take.at[source], out_send.at[there], out_recv.at[source], (c, there)
        )

    @pl.loop(1, EXPS)
    def _(d):
        out_copy(lax.rem(e + d, EXPS), e).start()

    half_rows, half_model = slots // 2, model // 2
    gathers, reduces = [], []
    for i in range(2):
        row = i * half_rows
        gathers.append(
            [
                PlaneGather(
                    chunk_part(rows_in, row, half_rows, h * half_model, half_model),
                    h == 0,
                    ag_send.at[i, h],
                    ag_recv.at[i, h],
                )
                for h in range(2)
            ]
        )

        def landing(i, h):
            def at(k, which):
                if which is None:
                    return late.at[i, h, k]
                return late.at[i, h, k, :, pl.ds(which * (half_model // 2), half_model // 2)]

            return at

        reduces.append(
            [
                PlaneReduce(
                    chunk_part(sums, row, half_rows, h * half_model, half_model),
                    landing(i, h),
                    h == 0,
                    rs_send.at[i, h],
                    rs_recv.at[i, h],
                )
                for h in range(2)
            ]
        )

    def collect(i):
        first = i * (EXPS // 2)

        @pl.loop(first, first + EXPS // 2)
        def _(j):
            @pl.when(j != e)
            def _():
                out_copy(e, j).wait_recv()

        for j in range(first, first + EXPS // 2):
            packed[pl.ds(j * CAP, CAP), :] = take[j].astype(f32)
        at = pl.ds(i * half_rows, half_rows)
        rows_in[c, at, :] = packed[at, :].astype(bf16)

    step = 512
    many = PLANE * half_rows

    def gate_up(i, begin, end):
        @pl.loop(begin, end)
        def _(k):
            at = pl.ds(pl.multiple_of(k * step, step), step)
            block = rows_in[:, pl.ds(i * half_rows, half_rows), at].reshape(many, step)
            acc_g[i] += lax.dot_general(block, wg[:, at], turned, preferred_element_type=f32)
            acc_u[i] += lax.dot_general(block, wu[:, at], turned, preferred_element_type=f32)

    def hidden_of(i):
        gate = acc_g[i]
        return ((gate / (1.0 + jnp.exp(-gate))) * acc_u[i]).astype(bf16)

    def down(i, hidden, begin, end):
        @pl.loop(begin, end)
        def _(k):
            at = pl.ds(pl.multiple_of(k * step, step), step)
            block = jnp.dot(hidden, wd[:, at], preferred_element_type=f32)
            sums[:, pl.ds(i * half_rows, half_rows), at] = block.astype(bf16).reshape(
                PLANE, half_rows, step
            )

    def give_back(i):
        for r in reduces[i]:
            r.close(4)
        packed[pl.ds(i * half_rows, half_rows), :] = sums[
            c, pl.ds(i * half_rows, half_rows), :
        ].astype(f32)
        first = i * (EXPS // 2)
        for j in range(first, first + EXPS // 2):
            back[j] = packed[pl.ds(j * CAP, CAP), :].astype(bf16)

        @pl.loop(first, first + EXPS // 2)
        def _(j):
            @pl.when(j != e)
            def _():
                back_copy(j, e).start()

            @pl.when(j == e)
            def _():
                ret[e] = back[e]

    def back_copy(there, source):
        return remote(
            back.at[there], ret.at[source], back_send.at[there], back_recv.at[source], (c, there)
        )

    first, second = gathers
    collect(0)
    first_sends(first)
    collect(1)
    first_sends(second)
    acc_g[...] = jnp.zeros_like(acc_g)
    acc_u[...] = jnp.zeros_like(acc_u)
    first_hop(first)
    first_hop(second)
    first_axis_done(first)
    first_axis_done(second)
    second_hop(first)
    second_axis_done(first)
    for load in loads:
        load.wait()
    steps = model // step
    for j in range(SIDE):
        gate_up(0, j * (steps // SIDE), (j + 1) * (steps // SIDE))
        second_hop_of(second, j)
    hidden = hidden_of(0)
    down(0, hidden, 0, steps)
    for j in range(SIDE):
        for r in reduces[0]:
            r.far(j)
    second_axis_done(second)
    for j in range(SIDE):
        gate_up(1, j * (steps // SIDE), (j + 1) * (steps // SIDE))
        for r in reduces[0]:
            r.near(j)
    hidden = hidden_of(1)
    down(1, hidden, 0, steps)
    for j in range(SIDE):
        for r in reduces[1]:
            r.far(j)
    for j in range(SIDE):
        for r in reduces[0]:
            r.close(j)
            if j == 0:
                r.far(4)
    for j in range(SIDE):
        for r in reduces[1]:
            r.near(j)
    for r in reduces[0]:
        r.near(4)
    for j in range(SIDE):
        for r in reduces[1]:
            r.close(j)
            if j == 0:
                r.far(4)
    give_back(0)
    for r in reduces[1]:
        r.near(4)
    give_back(1)

    @pl.loop(0, EXPS)
    def _(j):
        @pl.when(j != e)
        def _():
            back_copy(e, j).wait_recv()

    for j in range(EXPS):
        packed[pl.ds(j * CAP, CAP), :] = ret[j].astype(f32)
    moe = jnp.dot(combine[...], packed[...], preferred_element_type=f32, precision=precise)
    out[...] = (residual[...].astype(f32) + moe).astype(bf16)

    for pair in gathers:
        for g in pair:
            g.finish()
    for pair in reduces:
        for r in pair:
            r.finish()

    @pl.loop(1, EXPS)
    def _(d):
        there = lax.rem(e + d, EXPS)
        out_copy(there, e).wait_send()
        back_copy(there, e).wait_send()


def experts_of(normed, selector, combine, residual, wg, wu, wd):
    own, model = normed.shape
    slots = selector.shape[0]
    units = wg.shape[0]
    dma = pltpu.SemaphoreType.DMA
    vmem = pl.BlockSpec(memory_space=pltpu.VMEM)
    anywhere = pl.BlockSpec(memory_space=pltpu.HBM)
    pairs = pltpu.VMEM((EXPS, CAP, model), bf16)
    return pl.pallas_call(
        expert_kernel,
        out_shape=jax.ShapeDtypeStruct((own, model), bf16),
        in_specs=[vmem] * 4 + [anywhere] * 3,
        out_specs=vmem,
        scratch_shapes=[
            pltpu.VMEM((units, model), bf16),
            pltpu.VMEM((units, model), bf16),
            pltpu.VMEM((units, model), bf16),
            pairs,
            pairs,
            pairs,
            pairs,
            pltpu.VMEM((slots, model), f32),
            pltpu.VMEM((PLANE, slots, model), bf16),
            pltpu.VMEM((2, PLANE * slots // 2, units), f32),
            pltpu.VMEM((2, PLANE * slots // 2, units), f32),
            pltpu.VMEM((PLANE, slots, model), bf16),
            pltpu.VMEM((2, 2, 20, slots // 2, model // 2), bf16),
            dma((3,)),
            dma((EXPS,)),
            dma((EXPS,)),
            dma((EXPS,)),
            dma((EXPS,)),
            dma((2, 2, 20)),
            dma((2, 2, 20)),
            dma((2, 2, 20)),
            dma((2, 2, 20)),
        ],
        compiler_params=pltpu.CompilerParams(
            collective_id=1, has_side_effects=True, vmem_limit_bytes=62 << 20
        ),
        name="experts",
    )(normed, selector, combine, residual, wg, wu, wd)


def local(
    tokens,
    input_weight,
    gate_weight,
    conv_weight,
    conv_bias,
    state_weight,
    step_size,
    skip_gain,
    output_weight,
    norm_gain,
    router_weight,
    expert_gate,
    expert_up,
    expert_down,
    expert_ids,
):
    residual = mixer(
        tokens,
        input_weight,
        gate_weight,
        conv_weight,
        conv_bias,
        state_weight,
        step_size,
        skip_gain,
        output_weight,
    )
    row_count = expert_ids.shape[0]
    stream = residual.astype(f32)
    normed = (
        stream
        * lax.rsqrt(jnp.mean(stream * stream, -1, keepdims=True) + 1e-05)
        * norm_gain[None, :]
    ).astype(bf16)
    logits = jnp.dot(normed, router_weight, preferred_element_type=f32)
    experts = router_weight.shape[1]
    expert_range = jnp.arange(experts, dtype=jnp.int32)
    chosen = expert_ids[:, :, None] == expert_range[None, None, :]
    selected_entry = jnp.sum(jnp.where(chosen, logits[:, None, :], 0.0), -1)
    shares = jax.nn.sigmoid(selected_entry - selected_entry[:, ::-1])
    flat_hits = chosen.reshape(row_count * TOP, experts).astype(f32)
    earlier_hits = jnp.dot(
        jnp.tril(jnp.ones((row_count * TOP, row_count * TOP), f32), -1),
        flat_hits,
        precision=precise,
    )
    slot_index = jnp.sum(earlier_hits * flat_hits, -1).astype(jnp.int32)
    target = expert_ids.reshape(-1) * CAP + slot_index
    placed = target[:, None] == jnp.arange(experts * CAP, dtype=jnp.int32)[None, :]
    placed = placed.reshape(row_count, TOP, experts * CAP)
    selector = jnp.any(placed, 1).astype(bf16).T
    combine = jnp.sum(jnp.where(placed, shares[:, :, None], 0.0), 1)
    return experts_of(
        normed, selector, combine, residual, expert_gate[0], expert_up[0], expert_down[0]
    )


def solution(mesh):
    in_specs = (
        P("ctx", "exp"),
        P("ctx", "exp"),
        P("ctx", "exp"),
        P(None, "exp"),
        P("exp"),
        P("exp", None),
        P("ctx", "exp"),
        P("exp"),
        P("exp", "ctx"),
        P(),
        P(),
        P("exp", "ctx", None),
        P("exp", "ctx", None),
        P("exp", "ctx", None),
        P(("ctx", "exp"), None),
    )
    out_specs = P(("ctx", "exp"), None)
    return jax.shard_map(local, mesh=mesh, in_specs=in_specs, out_specs=out_specs, check_vma=False)
```

```python
import functools

import jax
import jax.numpy as jnp
from jax import lax
from jax.experimental import pallas as pl
from jax.experimental.pallas import tpu as pltpu
from jax.sharding import PartitionSpec as P

STATE = 16
CONV = 4
TOP = 2
CAP = 2
SIDE = 4
PLANE = SIDE * SIDE
DEPTH = 8
EXPS = 2 * DEPTH
CHUNK = 8

precise = lax.Precision.HIGHEST
f32 = jnp.float32
bf16 = jnp.bfloat16
MESH = pl.DeviceIdType.MESH


def remote(src, dst, send_sem, recv_sem, device):
    return pltpu.make_async_remote_copy(
        src_ref=src,
        dst_ref=dst,
        send_sem=send_sem,
        recv_sem=recv_sem,
        device_id=device,
        device_id_type=MESH,
    )


def all_sent(ref, sem):
    pltpu.make_async_copy(ref, ref, sem).wait()


def all_landed(ref, sem):
    pltpu.make_async_copy(ref, ref, sem).wait()


def greeting(*groups):
    barrier = pltpu.get_barrier_semaphore()
    for count, device_of in groups:

        @pl.loop(1, count)
        def _(d):
            pl.semaphore_signal(barrier, inc=1, device_id=device_of(d), device_id_type=MESH)

    return lambda: pl.semaphore_wait(barrier, sum(count - 1 for count, _ in groups))


class PlaneView:
    def __init__(self, x_first):
        c, self.e = lax.axis_index("ctx"), lax.axis_index("exp")
        y, x = c // SIDE, lax.rem(c, SIDE)
        self.x_first = x_first
        self.f, self.s = (x, y) if x_first else (y, x)

    def at(self, df, ds):
        f, s = lax.rem(self.f + df + SIDE, SIDE), lax.rem(self.s + ds + SIDE, SIDE)
        return s * SIDE + f if self.x_first else f * SIDE + s


class PlaneGather:
    ORDER = (0, -1, 1, 2)

    def __init__(self, part, x_first, send, recv):
        self.view, self.part, self.send, self.recv = PlaneView(x_first), part, send, recv

    def landing(self, k):
        if k < 4:
            return self.recv.at[min(k, 2)]
        j, kind = (k - 4) // 4, (k - 4) % 4
        return self.recv.at[3 + 2 * j + kind if kind < 2 else 11]

    def start(self, *ks):
        at = self.view.at
        for k in ks:
            kind = k % 4
            slot, which = ((0, None), (0, None), (-1, 0), (1, 1))[kind]
            to = 1 if kind % 2 == 0 else -1
            if k < 4:
                block, target = self.part(at(slot, 0), which), at(to, 0)
            else:
                block, target = self.part(at(self.ORDER[(k - 4) // 4], slot), which), at(0, to)
            remote(block, block, self.send, self.landing(k), (target, self.view.e)).start()

    def await_(self, k):
        all_landed(self.part(0, None), self.landing(k))

    def await_halves(self):
        all_landed(self.part(pl.ds(0, SIDE), None), self.recv.at[11])

    def finish(self, blocks):
        all_sent(blocks, self.send)


def first_sends(gathers):
    for g in gathers:
        g.start(0, 1)
    for g in gathers:
        g.start(4, 5)


def first_hop(gathers):
    for g in gathers:
        g.await_(0)
        g.start(2, 8, 9)
        g.await_(1)
        g.start(3, 12, 13)


def first_axis_done(gathers):
    for g in gathers:
        g.await_(2)
        g.start(16, 17)


def second_hop_of(gathers, j):
    for g in gathers:
        g.await_(4 + 4 * j)
        g.start(6 + 4 * j)
        g.await_(5 + 4 * j)
        g.start(7 + 4 * j)


def second_hop(gathers):
    for j in range(SIDE):
        second_hop_of(gathers, j)


def second_axis_done(gathers):
    for g in gathers:
        g.await_halves()


def rows_part(ref, begin, length):
    def part(slot, which):
        if which is None:
            return ref.at[slot, pl.ds(begin, length), :]
        return ref.at[slot, pl.ds(begin + which * (length // 2), length // 2), :]

    return part


def mix(
    tok,
    wx,
    wz,
    cw_hbm,
    cb_hbm,
    sw_hbm,
    ss,
    sg_hbm,
    wo,
    extra_loads,
    out,
    tg,
    gw,
    go,
    cw,
    cb,
    sw,
    sg,
    steps,
    acc,
    gate,
    ext,
    tail,
    halo,
    mw,
    keep,
    cum,
    read,
    q0,
    q1,
    q2,
    q3,
    sb,
    st,
    mg,
    ml,
    part,
    pair,
    summed,
    landed,
    leave,
    fin,
    town,
    stage,
    load_sem,
    tok_send,
    tok_recv,
    w_send,
    w_recv,
    ss_send,
    ss_recv,
    z_send,
    z_recv,
    core_send,
    core_recv,
    gw_send,
    gw_recv,
    go_send,
    go_recv,
    halo_send,
    halo_recv,
    q_send,
    q_recv,
    st_send,
    st_recv,
    mg_send,
    mg_recv,
    pair_send,
    pair_recv,
    sum_send,
    sum_recv,
    fin_send,
    fin_recv,
):
    c, e = lax.axis_index("ctx"), lax.axis_index("exp")
    y, x = c // SIDE, lax.rem(c, SIDE)
    z, core = e // 2, lax.rem(e, 2)
    partner = z * 2 + 1 - core
    rows, width = tok.shape
    lanes = wx.shape[1] // SIDE
    own_rows = out.shape[0]

    def around(value, size):
        return lax.rem(value + size, size)

    def first(ref, count):
        return ref.at[pl.ds(0, count)]

    def in_row(index):
        return y * SIDE + index // 2, z * 2 + lax.rem(index, 2)

    def along_z(d):
        return c, around(z + d, DEPTH) * 2 + core

    def along_y(d):
        return around(y + d, SIDE) * SIDE + x, e

    def along_x(d):
        return y * SIDE + around(x + d, SIDE), e

    spot = x * 2 + core
    spots = 2 * SIDE
    meet = greeting(
        (SIDE, along_x),
        (SIDE, along_y),
        (2, lambda d: along_z(d)),
        (2, lambda d: along_z(-d)),
        (2, lambda d: (c, partner)),
    )

    def columns(block):
        return pl.ds(pl.multiple_of(block * lanes, lanes), lanes)

    mine = columns(x)
    loads = [
        pltpu.make_async_copy(source, place, load_sem.at[i])
        for i, (source, place) in enumerate(
            (
                (tok, tg.at[e, x]),
                (wx.at[:, mine], gw.at[c, :, pl.ds(0, lanes)]),
                (wz.at[:, mine], gw.at[c, :, pl.ds(lanes, lanes)]),
                (ss.at[:, mine], steps.at[x]),
                (cw_hbm.at[:, mine], cw),
                (cb_hbm.at[:, mine], cb),
                (sw_hbm.at[:, mine], sw),
                (sg_hbm.at[:, mine], sg),
                (wo, go.at[y]),
            )
        )
    ]
    for load in loads:
        load.start()
    for load in extra_loads:
        load.start()
    meet()

    def tok_part(slot, which):
        s = slot if isinstance(slot, int) else lax.rem(slot, SIDE)
        return tg.at[e, s] if which is None else tg.at[e, s, pl.ds(which * (rows // 2), rows // 2), :]

    row_tokens = PlaneGather(tok_part, True, tok_send, tok_recv)
    deep = gw.shape[1] // 2
    sides = (pl.ds(0, lanes), pl.ds(lanes, lanes))

    def own_channels(d, part_of, place, k):
        to = columns(around(x + d, SIDE))
        hop = d if part_of is None else (1, -1)[part_of]
        at = pl.ds(0, 2 * deep) if part_of is None else pl.ds(part_of * deep, deep)
        for weight, side in zip((wx, wz), sides, strict=True):
            remote(weight.at[at, to], place.at[:, side], w_send, w_recv.at[k], along_x(hop)).start()

    for load in loads[:3]:
        load.wait()
    row_tokens.start(0, 1)

    def z_part(zz, s, which):
        slot = around(zz, DEPTH) * 2 + core
        if which is None:
            return tg.at[slot, s]
        return tg.at[slot, s, pl.ds(which * (rows // 2), rows // 2), :]

    def z_copy(way, hop, s):
        block = z - (hop - 1) if way == 0 else z + (hop - 1)
        ref = z_part(block, s, None if hop < 4 else way)
        to = around(z + (1 if way == 0 else -1), DEPTH) * 2 + core
        return remote(ref, ref, z_send, z_recv.at[hop - 1, s], (c, to))

    def z_start(hop, s):
        for way in range(2):
            z_copy(way, hop, s).start()

    def core_copy(zz):
        ref = tg.at[zz * 2 + core]
        return remote(ref, ref, core_send, core_recv, (c, partner))

    order = [around(x + d, SIDE) for d in PlaneGather.ORDER]
    weights = PlaneGather(
        rows_part(gw, 0, gw.shape[1]), True, gw_send, gw_recv
    )
    own_channels(1, None, gw.at[c], 0)
    own_channels(-1, None, gw.at[c], 1)
    own_channels(2, 0, stage.at[0], 3)
    own_channels(2, 1, stage.at[1], 4)
    z_start(1, order[0])
    weights.start(4, 5)
    row_tokens.await_(0)
    row_tokens.start(2)
    z_start(1, order[1])
    row_tokens.await_(1)
    row_tokens.start(3)
    z_start(1, order[2])
    for way in range(2):
        all_landed(stage.at[way], w_recv.at[3 + way])
        place = gw.at[y * SIDE + order[1 + way], pl.ds(way * deep, deep), :]
        remote(stage.at[way], place, w_send, w_recv.at[2], along_x((1, -1)[way])).start()
    for i in range(2):
        all_landed(gw.at[0], w_recv.at[i])
        weights.start(8 + 4 * i, 9 + 4 * i)
    row_tokens.await_(2)
    z_start(1, order[3])
    core_copy(z).start()
    all_landed(gw.at[0], w_recv.at[2])
    weights.start(16, 17)
    for d in (1, 3, 2):
        theirs = columns(around(x + d, SIDE))
        remote(ss.at[:, theirs], steps.at[x], ss_send, ss_recv, along_x(d)).start()

    def z_hop(hop):
        for s in order:
            if hop < 4:
                all_landed(tg.at[0, pl.ds(0, 2)], z_recv.at[hop - 1, s])
                z_start(hop + 1, s)
            else:
                all_landed(tg.at[0, 0], z_recv.at[hop - 1, s])
        core_copy(around(z - hop, DEPTH)).start()
        if hop < 4:
            core_copy(around(z + hop, DEPTH)).start()

    second_hop_of((weights,), 0)
    z_hop(1)
    second_hop_of((weights,), 1)
    second_hop_of((weights,), 2)
    z_hop(2)
    second_hop_of((weights,), 3)
    z_hop(3)
    second_axis_done((weights,))
    outs = PlaneGather(
        lambda slot, which: go.at[slot // SIDE]
        if which is None
        else go.at[slot // SIDE, pl.ds(which * (go.shape[1] // 2), go.shape[1] // 2), :],
        False,
        go_send,
        go_recv,
    )
    for load in loads[3:]:
        load.wait()
    outs.start(0, 1)
    all_landed(first(steps, SIDE - 1), ss_recv)
    keep[...] = jnp.exp(-jnp.concatenate([steps[s] for s in range(SIDE)], axis=1))
    z_hop(4)

    all_landed(first(tg, DEPTH), core_recv)

    acc[...] = jnp.zeros_like(acc)
    many = SIDE * rows

    @pl.loop(0, EXPS)
    def _(j):
        acc[...] += jnp.dot(tg[j].reshape(many, width), gw[j], preferred_element_type=f32)

    held = halo.shape[0]
    tail[...] = acc[pl.ds(many - held, held), pl.ds(0, lanes)].astype(bf16)

    def halo_copy():
        return remote(tail, halo, halo_send, halo_recv, along_y(1))

    @pl.when(y < SIDE - 1)
    def _():
        halo_copy().start()

    for s in range(SIDE):
        at = pl.ds(s * lanes, lanes)
        here = pl.ds(s * rows, rows)
        ext[pl.ds(held, rows), at] = acc[here, pl.ds(0, lanes)].astype(bf16).astype(f32)
        gate[:, at] = acc[here, pl.ds(lanes, lanes)].astype(bf16).astype(f32)
        if s:
            ext[pl.ds(0, held), at] = ext[pl.ds(rows, held), pl.ds((s - 1) * lanes, lanes)]

    @pl.when(y == 0)
    def _():
        halo[...] = jnp.zeros_like(halo)

    @pl.when(y > 0)
    def _():
        halo_copy().wait_recv()

    ext[pl.ds(0, held), pl.ds(0, lanes)] = halo[...].astype(f32)

    def spread(values):
        return jnp.concatenate([values] * SIDE, axis=1)

    filtered = jnp.broadcast_to(spread(cb[...]), keep.shape)
    for offset in range(CONV):
        begin = held - (CONV - 1) + offset
        tap = spread(cw[pl.ds(offset, 1), :])
        filtered = filtered + tap * ext[pl.ds(begin, rows), :]
    mixer_in = (filtered / (1.0 + jnp.exp(-filtered))).astype(bf16)
    mw[...] = mixer_in.astype(f32)

    for s in range(SIDE):
        both = lax.dot_general(
            sw[...],
            mixer_in[:, s * lanes : (s + 1) * lanes],
            (((1,), (1,)), ((), ())),
            preferred_element_type=f32,
        )
        q0[2 * s] = both[:STATE]
        q0[2 * s + 1] = both[STATE:]

    def to_sum(source, there):
        return remote(
            q0.at[there], q1.at[source], q_send.at[0], q_recv.at[0], in_row(there)
        )

    def z_sum(d, source):
        return remote(q2.at[source], q2.at[source], q_send.at[1], q_recv.at[1], along_z(d))

    def to_share(source, there):
        return remote(
            q3.at[source], q3.at[source], q_send.at[2], q_recv.at[2], in_row(there)
        )

    @pl.loop(1, spots)
    def _(d):
        to_sum(spot, around(spot + d, spots)).start()

    q1[spot] = q0[spot]
    outs.await_(0)
    outs.start(2)
    outs.await_(1)
    outs.start(3)

    picked = lax.broadcasted_iota(jnp.int32, (own_rows, rows), 1) == (
        lax.broadcasted_iota(jnp.int32, (own_rows, rows), 0) + e * own_rows
    )
    picker = picked.astype(f32).astype(bf16)

    @pl.loop(0, EXPS)
    def _(j):
        town[j] = jnp.dot(picker, tg[j, x], preferred_element_type=f32)

    all_landed(first(q1, spots - 1), q_recv.at[0])

    total = q1[0]
    for j in range(1, spots):
        total = total + q1[j]
    q2[z] = total

    @pl.loop(1, DEPTH)
    def _(d):
        z_sum(d, z).start()

    all_landed(first(q2, DEPTH - 1), q_recv.at[1])

    total = q2[0]
    for j in range(1, DEPTH):
        total = total + q2[j]
    q3[spot] = total

    @pl.loop(1, spots)
    def _(d):
        to_share(spot, around(spot + d, spots)).start()

    all_landed(first(q3, spots - 1), q_recv.at[2])

    chunks = rows // CHUNK
    for k in range(2):
        for s in range(SIDE):
            vectors = q3[2 * s + k]
            for j in range(chunks):
                sb[j, pl.ds(k * STATE, STATE), pl.ds(s * CHUNK, CHUNK)] = vectors[
                    :, j * CHUNK : (j + 1) * CHUNK
                ]

    def advance(j, carry):
        state, decay = carry
        vectors = sb[j]
        first = pl.multiple_of(j * CHUNK, CHUNK)
        keeps, inputs = keep[pl.ds(first, CHUNK), :], mw[pl.ds(first, CHUNK), :]

        def vector(begin, i):
            picks = [
                jnp.broadcast_to(
                    vectors[begin : begin + STATE, s * CHUNK + i : s * CHUNK + i + 1],
                    (STATE, lanes),
                )
                for s in range(SIDE)
            ]
            return jnp.concatenate(picks, axis=1)

        for i in range(CHUNK):
            kept = keeps[i : i + 1, :]
            state = kept * state + inputs[i : i + 1, :] * vector(0, i)
            decay = decay * kept
            read[pl.ds(first + i, 1), :] = jnp.sum(
                vector(STATE, i) * state, axis=0, keepdims=True
            )
            cum[pl.ds(first + i, 1), :] = decay
        return state, decay

    wide = SIDE * lanes
    state, decay = lax.fori_loop(
        0, chunks, advance, (jnp.zeros((STATE, wide), f32), jnp.ones((1, wide), f32))
    )

    ends = [state[:, s * lanes : (s + 1) * lanes] for s in range(SIDE)]
    keeps = [decay[:, s * lanes : (s + 1) * lanes] for s in range(SIDE)]
    row_end, row_keep = ends[0], keeps[0]
    for s in range(1, SIDE):
        row_end, row_keep = keeps[s] * row_end + ends[s], keeps[s] * row_keep
    st[y, pl.ds(0, STATE), :] = row_end
    st[y, pl.ds(STATE, 8), :] = jnp.broadcast_to(row_keep, (8, lanes))

    def st_copy(d, slot):
        return remote(st.at[slot], st.at[slot], st_send.at[d], st_recv.at[d], along_y(d))

    @pl.loop(1, SIDE - y)
    def _(d):
        st_copy(d, y).start()

    gated = gate[...] / (1.0 + jnp.exp(-gate[...]))
    inside = read[...] + spread(sg[...]) * mw[...]

    def enter(source, entering):
        st_copy(y - source, source).wait_recv()
        return st[source, pl.ds(STATE, 1), :] * entering + st[source, pl.ds(0, STATE), :]

    entering = lax.fori_loop(0, y, enter, jnp.zeros((STATE, lanes), f32))
    carried = []
    for s in range(SIDE):
        carried.append(
            lax.dot_general(
                q3[2 * s + 1],
                entering,
                (((0,), (0,)), ((), ())),
                preferred_element_type=f32,
                precision=precise,
            )
        )
        entering = keeps[s] * entering + ends[s]
    mixed = (inside + cum[...] * jnp.concatenate(carried, axis=1)) * gated
    for s in range(SIDE):
        mg[x, s] = mixed[:, s * lanes : (s + 1) * lanes].astype(bf16)

    def mg_part(slot, which):
        at = slot if isinstance(slot, int) else lax.rem(slot, SIDE)
        return mg.at[at] if which is None else mg.at[at, pl.ds(which * 2, 2)]

    channels = PlaneGather(mg_part, True, mg_send, mg_recv)
    channels.start(0, 1)
    outs.await_(2)
    channels.await_(0)
    channels.start(2)
    channels.await_(1)
    channels.start(3)
    channels.await_(2)
    for s in range(SIDE):
        ml[:, pl.ds(s * lanes, lanes)] = mg[s].reshape(many, lanes)

    block_columns = go.shape[2]
    halves = [pl.ds(h * 2 * block_columns, 2 * block_columns) for h in range(2)]

    def pair_copy(h):
        return remote(
            part.at[1 - core, :, :, :, halves[h]],
            pair.at[:, :, :, halves[h]],
            pair_send.at[h],
            pair_recv.at[h],
            (c, partner),
        )

    def sum_copy(h, d, there, source):
        return remote(
            summed.at[there, :, :, halves[h]],
            landed.at[source, :, :, halves[h]],
            sum_send.at[h],
            sum_recv.at[h],
            along_z(d),
        )

    def both_cores(h, there):
        at = halves[h]
        return part[core, there, :, :, at].astype(f32) + pair[there, :, :, at].astype(f32)

    for h in range(2):

        @pl.loop(2 * h, 2 * h + 2)
        def _(j):
            block = jnp.dot(ml[...], go[j], preferred_element_type=f32)
            at = pl.ds(pl.multiple_of(j * block_columns, block_columns), block_columns)
            for i in range(EXPS):
                for s in range(SIDE):
                    begin = s * rows + i * own_rows
                    part[i % 2, i // 2, s, :, at] = block[begin : begin + own_rows].astype(bf16)

        pair_copy(h).start()
    for h in range(2):
        pair_copy(h).wait_recv()

        @pl.loop(1, DEPTH)
        def _(d):
            there = around(z + d, DEPTH)
            summed[there, :, :, halves[h]] = both_cores(h, there).astype(bf16)
            sum_copy(h, d, there, z).start()

    for h in range(2):

        def collect(d, total):
            return total + landed[around(z - d, DEPTH), :, :, halves[h]].astype(f32)

        all_landed(landed.at[pl.ds(0, DEPTH - 1), :, :, halves[h]], sum_recv.at[h])
        total = lax.fori_loop(1, DEPTH, collect, both_cores(h, z))
        leave[:, :, halves[h]] = total.astype(bf16)

    def fin_copy(there, source):
        return remote(
            leave.at[there], fin.at[source], fin_send, fin_recv, (y * SIDE + there, e)
        )

    for d in (1, 3, 2):
        fin_copy(around(x + d, SIDE), x).start()
    fin[x] = leave[x]
    all_landed(first(fin, SIDE - 1), fin_recv)
    for i in range(SIDE):
        for s in range(SIDE):
            block = i * SIDE + s
            term = fin[s, :, pl.ds(i * block_columns, block_columns)].astype(f32)
            out[:, pl.ds(block * width, width)] = (town[block] + term).astype(bf16)

    row_tokens.finish(tg.at[e, pl.ds(0, SIDE - 1)])
    all_sent(first(gw, SIDE), w_send)
    all_sent(first(steps, SIDE - 1), ss_send)
    all_sent(first(tg, DEPTH - 1), z_send)
    all_sent(first(tg, DEPTH), core_send)
    weights.finish(first(gw, 12))
    outs.finish(first(go, SIDE - 1))
    channels.finish(first(mg, SIDE - 1))
    all_sent(first(q0, spots - 1), q_send.at[0])
    all_sent(first(q2, DEPTH - 1), q_send.at[1])
    all_sent(first(q3, spots - 1), q_send.at[2])
    for h in range(2):
        all_sent(summed.at[pl.ds(0, DEPTH - 1), :, :, halves[h]], sum_send.at[h])
        pair_copy(h).wait_send()
    all_sent(first(leave, SIDE - 1), fin_send)

    @pl.when(y < SIDE - 1)
    def _():
        halo_copy().wait_send()

    @pl.loop(1, SIDE - y)
    def _(d):
        st_copy(d, y).wait_send()


def mix_scratch(rows, width, depth, inner):
    lanes = inner // SIDE
    model = width * EXPS
    own = rows // EXPS
    dma = pltpu.SemaphoreType.DMA
    vmem = pltpu.VMEM
    wide = vmem((rows, inner), f32)
    spread = (DEPTH, SIDE, own, model // SIDE)
    vectors = vmem((2 * SIDE, STATE, rows), f32)
    return [
        vmem((EXPS, SIDE, rows, width), bf16),
        vmem((PLANE, depth, 2 * lanes), bf16),
        vmem((SIDE, inner, width), bf16),
        vmem((CONV, lanes), f32),
        vmem((1, lanes), f32),
        vmem((2 * STATE, lanes), bf16),
        vmem((1, lanes), f32),
        vmem((SIDE, rows, lanes), f32),
        vmem((SIDE * rows, 2 * lanes), f32),
        wide,
        vmem((rows + 16, inner), f32),
        vmem((16, lanes), bf16),
        vmem((16, lanes), bf16),
        wide,
        wide,
        wide,
        wide,
        vectors,
        vectors,
        vmem((DEPTH, STATE, rows), f32),
        vectors,
        vmem((rows // CHUNK, 2 * STATE, 128), f32),
        vmem((SIDE, STATE + 8, lanes), f32),
        vmem((SIDE, SIDE, rows, lanes), bf16),
        vmem((SIDE * rows, inner), bf16),
        vmem((2, *spread), bf16),
        vmem(spread, bf16),
        vmem(spread, bf16),
        vmem(spread, bf16),
        vmem(spread[1:], bf16),
        vmem(spread[1:], bf16),
        vmem((EXPS, own, width), f32),
        vmem((2, depth // 2, 2 * lanes), bf16),
        dma((9,)),
        dma,
        dma((3,)),
        dma,
        dma((5,)),
        dma,
        dma,
        dma,
        dma((4, SIDE)),
        dma,
        dma,
        dma,
        dma((12,)),
        dma,
        dma((3,)),
        dma,
        dma,
        dma((3,)),
        dma((3,)),
        dma((SIDE,)),
        dma((SIDE,)),
        dma,
        dma((3,)),
        dma((2,)),
        dma((2,)),
        dma((2,)),
        dma((2,)),
        dma,
        dma,
    ]


class PlaneReduce:
    ORDER = (2, -1, 1, 0)

    def __init__(self, part, late, x_first, send, recv):
        self.view, self.part, self.late = PlaneView(x_first), part, late
        self.send, self.recv = send, recv

    def mine(self, j, step, which):
        at = self.view.at
        return self.part(at(self.ORDER[j], step) if j < 4 else at(step, 0), which)

    def start(self, k):
        j, kind = k // 4, k % 4
        step, which, to = ((2, 0, 1), (2, 1, -1), (1, None, 1), (-1, None, -1))[kind]
        target = self.view.at(0, to) if j < 4 else self.view.at(to, 0)
        source, place = self.mine(j, step, which), self.late(k, which)
        remote(source, place, self.send, self.recv.at[k // 2], (target, self.view.e)).start()

    def far(self, j):
        self.start(4 * j)
        self.start(4 * j + 1)

    def near(self, j):
        all_landed(self.late(4 * j, None), self.recv.at[2 * j])
        for kind, step in ((0, 1), (1, -1)):
            mine, came = self.mine(j, step, kind), self.late(4 * j + kind, kind)
            mine[...] = (mine[...].astype(f32) + came[...].astype(f32)).astype(bf16)
            self.start(4 * j + 2 + kind)

    def close(self, j):
        all_landed(self.late(pl.ds(4 * j + 2, 2), None), self.recv.at[2 * j + 1])
        mine, first, second = self.mine(j, 0, None), self.late(4 * j + 2, None), self.late(4 * j + 3, None)
        total = first[...].astype(f32) + second[...].astype(f32)
        mine[...] = (mine[...].astype(f32) + total).astype(bf16)

    def finish(self):
        all_sent(self.part(pl.ds(0, 15), None), self.send)


def chunk_part(ref, row, rows, column, columns):
    def part(slot, which):
        if which is None:
            return ref.at[slot, pl.ds(row, rows), pl.ds(column, columns)]
        half = columns // 2
        return ref.at[slot, pl.ds(row, rows), pl.ds(column + which * half, half)]

    return part


def route(residual, norm_gain, router, ids):
    stream = residual[...].astype(f32)
    scale = lax.rsqrt(jnp.mean(stream * stream, axis=1, keepdims=True) + 1e-05)
    normed = (stream * scale * norm_gain[...]).astype(bf16)
    logits = lax.dot_general(
        router[...], normed, (((1,), (1,)), ((), ())), preferred_element_type=f32
    )
    experts, rows = logits.shape
    expert = lax.broadcasted_iota(jnp.int32, (experts, rows), 0)
    slot = lax.broadcasted_iota(jnp.int32, (experts * CAP, rows), 0).astype(f32)
    before = lax.broadcasted_iota(jnp.int32, (rows, rows), 0) < lax.broadcasted_iota(
        jnp.int32, (rows, rows), 1
    )
    named = [ids[pl.ds(k, 1), :] for k in range(TOP)]
    hits = [(expert == one).astype(f32) for one in named]
    earlier = jnp.dot(
        hits[0] + hits[1], before.astype(f32), preferred_element_type=f32, precision=precise
    )
    picked = [jnp.sum(hit * logits, axis=0, keepdims=True) for hit in hits]
    selector = jnp.zeros(slot.shape, f32)
    combine = jnp.zeros(slot.shape, f32)
    for k in range(TOP):
        rank = jnp.sum(hits[k] * earlier, axis=0, keepdims=True)
        placed = (slot == named[k].astype(f32) * CAP + rank).astype(f32)
        share = 1.0 / (1.0 + jnp.exp(picked[1 - k] - picked[k]))
        selector = selector + placed
        combine = combine + placed * share
    return normed, selector.astype(bf16), combine


def run_experts(
    residual,
    norm_gain,
    router,
    ids,
    loads,
    out,
    wg,
    wu,
    wd,
    give,
    take,
    back,
    ret,
    packed,
    rows_in,
    acc_g,
    acc_u,
    sums,
    late,
    out_send,
    out_recv,
    back_send,
    back_recv,
    ag_send,
    ag_recv,
    rs_send,
    rs_recv,
):
    c, e = lax.axis_index("ctx"), lax.axis_index("exp")
    slots, model = packed.shape
    turned = (((1,), (1,)), ((), ()))

    for load in loads[3:]:
        load.wait()
    normed, selector, combine = route(residual, norm_gain, router, ids)
    packed[...] = jnp.dot(selector, normed, preferred_element_type=f32)
    for j in range(EXPS):
        give[j] = packed[pl.ds(j * CAP, CAP), :].astype(bf16)
    take[e] = give[e]

    def out_copy(there, source):
        return remote(
            give.at[there], take.at[source], out_send, out_recv.at[source // (EXPS // 2)], (c, there)
        )

    @pl.loop(1, EXPS)
    def _(d):
        out_copy(lax.rem(e + d, EXPS), e).start()

    half_rows, half_model = slots // 2, model // 2
    gathers, reduces = [], []
    for i in range(2):
        row = i * half_rows
        gathers.append(
            [
                PlaneGather(
                    chunk_part(rows_in, row, half_rows, h * half_model, half_model),
                    h == 0,
                    ag_send.at[i, h],
                    ag_recv.at[i, h],
                )
                for h in range(2)
            ]
        )

        def landing(i, h):
            def at(k, which):
                if which is None:
                    return late.at[i, h, k]
                return late.at[i, h, k, :, pl.ds(which * (half_model // 2), half_model // 2)]

            return at

        reduces.append(
            [
                PlaneReduce(
                    chunk_part(sums, row, half_rows, h * half_model, half_model),
                    landing(i, h),
                    h == 0,
                    rs_send.at[i, h],
                    rs_recv.at[i, h],
                )
                for h in range(2)
            ]
        )

    def collect(i):
        first = i * (EXPS // 2)

        @pl.when(e // (EXPS // 2) == i)
        def _():
            all_landed(take.at[pl.ds(0, EXPS // 2 - 1)], out_recv.at[i])

        @pl.when(e // (EXPS // 2) != i)
        def _():
            all_landed(take.at[pl.ds(0, EXPS // 2)], out_recv.at[i])

        for j in range(first, first + EXPS // 2):
            packed[pl.ds(j * CAP, CAP), :] = take[j].astype(f32)
        at = pl.ds(i * half_rows, half_rows)
        rows_in[c, at, :] = packed[at, :].astype(bf16)

    step = 512
    many = PLANE * half_rows

    def gate_up(i, begin, end):
        @pl.loop(begin, end)
        def _(k):
            at = pl.ds(pl.multiple_of(k * step, step), step)
            block = rows_in[:, pl.ds(i * half_rows, half_rows), at].reshape(many, step)
            acc_g[i] += lax.dot_general(block, wg[:, at], turned, preferred_element_type=f32)
            acc_u[i] += lax.dot_general(block, wu[:, at], turned, preferred_element_type=f32)

    def hidden_of(i):
        gate = acc_g[i]
        return ((gate / (1.0 + jnp.exp(-gate))) * acc_u[i]).astype(bf16)

    def down(i, hidden, begin, end):
        @pl.loop(begin, end)
        def _(k):
            at = pl.ds(pl.multiple_of(k * step, step), step)
            block = jnp.dot(hidden, wd[:, at], preferred_element_type=f32)
            sums[:, pl.ds(i * half_rows, half_rows), at] = block.astype(bf16).reshape(
                PLANE, half_rows, step
            )

    def give_back(i):
        for r in reduces[i]:
            r.close(4)
        packed[pl.ds(i * half_rows, half_rows), :] = sums[
            c, pl.ds(i * half_rows, half_rows), :
        ].astype(f32)
        first = i * (EXPS // 2)
        for j in range(first, first + EXPS // 2):
            back[j] = packed[pl.ds(j * CAP, CAP), :].astype(bf16)

        @pl.loop(first, first + EXPS // 2)
        def _(j):
            @pl.when(j != e)
            def _():
                back_copy(j, e).start()

            @pl.when(j == e)
            def _():
                ret[e] = back[e]

    def back_copy(there, source):
        return remote(
            back.at[there], ret.at[source], back_send, back_recv, (c, there)
        )

    first, second = gathers
    collect(0)
    first_sends(first)
    collect(1)
    first_sends(second)
    acc_g[...] = jnp.zeros_like(acc_g)
    acc_u[...] = jnp.zeros_like(acc_u)
    first_hop(first)
    first_hop(second)
    first_axis_done(first)
    first_axis_done(second)
    second_hop(first)
    second_axis_done(first)
    for load in loads[:3]:
        load.wait()
    steps = model // step
    for j in range(SIDE):
        gate_up(0, j * (steps // SIDE), (j + 1) * (steps // SIDE))
        second_hop_of(second, j)
    hidden = hidden_of(0)
    down(0, hidden, 0, steps)
    for j in range(SIDE):
        for r in reduces[0]:
            r.far(j)
    second_axis_done(second)
    for j in range(SIDE):
        gate_up(1, j * (steps // SIDE), (j + 1) * (steps // SIDE))
        for r in reduces[0]:
            r.near(j)
    hidden = hidden_of(1)
    down(1, hidden, 0, steps)
    for j in range(SIDE):
        for r in reduces[1]:
            r.far(j)
    for j in range(SIDE):
        for r in reduces[0]:
            r.close(j)
            if j == 0:
                r.far(4)
    for j in range(SIDE):
        for r in reduces[1]:
            r.near(j)
    for r in reduces[0]:
        r.near(4)
    for j in range(SIDE):
        for r in reduces[1]:
            r.close(j)
            if j == 0:
                r.far(4)
    give_back(0)
    for r in reduces[1]:
        r.near(4)
    give_back(1)

    all_landed(ret.at[pl.ds(0, EXPS - 1)], back_recv)
    for j in range(EXPS):
        packed[pl.ds(j * CAP, CAP), :] = ret[j].astype(f32)
    moe = lax.dot_general(
        combine,
        packed[...],
        (((0,), (0,)), ((), ())),
        preferred_element_type=f32,
        precision=precise,
    )
    out[...] = (residual[...].astype(f32) + moe).astype(bf16)

    for pair in gathers:
        for g in pair:
            g.finish(g.part(pl.ds(0, 15), None))
    for pair in reduces:
        for r in pair:
            r.finish()
    all_sent(give.at[pl.ds(0, EXPS - 1)], out_send)
    all_sent(back.at[pl.ds(0, EXPS - 1)], back_send)


def expert_scratch(units, model):
    slots = EXPS * CAP
    dma = pltpu.SemaphoreType.DMA
    vmem = pltpu.VMEM
    weight = vmem((units, model), bf16)
    pairs = vmem((EXPS, CAP, model), bf16)
    return [
        weight,
        weight,
        weight,
        pairs,
        pairs,
        pairs,
        pairs,
        vmem((slots, model), f32),
        vmem((PLANE, slots, model), bf16),
        vmem((2, PLANE * slots // 2, units), f32),
        vmem((2, PLANE * slots // 2, units), f32),
        vmem((PLANE, slots, model), bf16),
        vmem((2, 2, 20, slots // 2, model // 2), bf16),
        dma,
        dma((2,)),
        dma,
        dma,
        dma((2, 2)),
        dma((2, 2, 12)),
        dma((2, 2)),
        dma((2, 2, 10)),
    ]


def layer_kernel(mix_count, *refs):
    mix_ins, (gain_hbm, router_hbm, wg_hbm, wu_hbm, wd_hbm, ids_hbm), out = refs[:9], refs[9:15], refs[15]
    residual, gain, router, ids, load_sem = refs[16:21]
    mix_refs, expert_refs = refs[21 : 21 + mix_count], refs[21 + mix_count :]
    loads = [
        pltpu.make_async_copy(source, place, load_sem.at[i])
        for i, (source, place) in enumerate(
            zip(
                (wg_hbm, wu_hbm, wd_hbm, gain_hbm, router_hbm, ids_hbm),
                (*expert_refs[:3], gain, router, ids),
                strict=True,
            )
        )
    ]
    mix(*mix_ins, loads, residual, *mix_refs)
    run_experts(residual, gain, router, ids, loads, out, *expert_refs)


def local(
    tokens,
    input_weight,
    gate_weight,
    conv_weight,
    conv_bias,
    state_weight,
    step_size,
    skip_gain,
    output_weight,
    norm_gain,
    router_weight,
    expert_gate,
    expert_up,
    expert_down,
    expert_ids,
):
    own, model = expert_ids.shape[0], norm_gain.shape[0]
    units, experts = expert_gate.shape[1], router_weight.shape[1]
    scratch = mix_scratch(*tokens.shape, *input_weight.shape)
    vmem = pltpu.VMEM
    return pl.pallas_call(
        functools.partial(layer_kernel, len(scratch)),
        out_shape=jax.ShapeDtypeStruct((own, model), bf16),
        in_specs=[pl.BlockSpec(memory_space=pltpu.HBM)] * 15,
        out_specs=pl.BlockSpec(memory_space=pltpu.VMEM),
        scratch_shapes=[
            vmem((own, model), bf16),
            vmem((1, model), f32),
            vmem((experts, model), bf16),
            vmem((TOP, own), jnp.int32),
            pltpu.SemaphoreType.DMA((6,)),
            *scratch,
            *expert_scratch(units, model),
        ],
        compiler_params=pltpu.CompilerParams(
            collective_id=0, has_side_effects=True, vmem_limit_bytes=62 << 20
        ),
        name="layer",
    )(
        tokens,
        input_weight,
        gate_weight,
        conv_weight,
        conv_bias.reshape(1, -1),
        state_weight.T,
        step_size,
        skip_gain.reshape(1, -1),
        output_weight,
        norm_gain.reshape(1, -1),
        router_weight.T,
        expert_gate[0],
        expert_up[0],
        expert_down[0],
        expert_ids.T,
    )


def solution(mesh):
    in_specs = (
        P("ctx", "exp"),
        P("ctx", "exp"),
        P("ctx", "exp"),
        P(None, "exp"),
        P("exp"),
        P("exp", None),
        P("ctx", "exp"),
        P("exp"),
        P("exp", "ctx"),
        P(),
        P(),
        P("exp", "ctx", None),
        P("exp", "ctx", None),
        P("exp", "ctx", None),
        P(("ctx", "exp"), None),
    )
    out_specs = P(("ctx", "exp"), None)
    return jax.shard_map(local, mesh=mesh, in_specs=in_specs, out_specs=out_specs, check_vma=False)
```

```python
import functools

import jax
import jax.numpy as jnp
from jax import lax
from jax.experimental import pallas as pl
from jax.experimental.pallas import tpu as pltpu
from jax.sharding import PartitionSpec as P

STATE = 16
CONV = 4
TOP = 2
CAP = 2
SIDE = 4
PLANE = SIDE * SIDE
DEPTH = 8
EXPS = 2 * DEPTH
CHUNK = 8

precise = lax.Precision.HIGHEST
f32 = jnp.float32
bf16 = jnp.bfloat16
MESH = pl.DeviceIdType.MESH


def remote(src, dst, send_sem, recv_sem, device):
    return pltpu.make_async_remote_copy(
        src_ref=src,
        dst_ref=dst,
        send_sem=send_sem,
        recv_sem=recv_sem,
        device_id=device,
        device_id_type=MESH,
    )


def all_sent(ref, sem):
    pltpu.make_async_copy(ref, ref, sem).wait()


def all_landed(ref, sem):
    pltpu.make_async_copy(ref, ref, sem).wait()


def greeting(*groups):
    barrier = pltpu.get_barrier_semaphore()
    for count, device_of in groups:

        @pl.loop(1, count)
        def _(d):
            pl.semaphore_signal(barrier, inc=1, device_id=device_of(d), device_id_type=MESH)

    return lambda: pl.semaphore_wait(barrier, sum(count - 1 for count, _ in groups))


class PlaneView:
    def __init__(self, x_first):
        c, self.e = lax.axis_index("ctx"), lax.axis_index("exp")
        y, x = c // SIDE, lax.rem(c, SIDE)
        self.x_first = x_first
        self.f, self.s = (x, y) if x_first else (y, x)

    def at(self, df, ds):
        f, s = lax.rem(self.f + df + SIDE, SIDE), lax.rem(self.s + ds + SIDE, SIDE)
        return s * SIDE + f if self.x_first else f * SIDE + s


class PlaneGather:
    ORDER = (0, -1, 1, 2)

    def __init__(self, part, x_first, send, recv):
        self.view, self.part, self.send, self.recv = PlaneView(x_first), part, send, recv

    def landing(self, k):
        if k < 4:
            return self.recv.at[min(k, 2)]
        j, kind = (k - 4) // 4, (k - 4) % 4
        return self.recv.at[3 + 2 * j + kind if kind < 2 else 11]

    def start(self, *ks):
        at = self.view.at
        for k in ks:
            kind = k % 4
            slot, which = ((0, None), (0, None), (-1, 0), (1, 1))[kind]
            to = 1 if kind % 2 == 0 else -1
            if k < 4:
                block, target = self.part(at(slot, 0), which), at(to, 0)
            else:
                block, target = self.part(at(self.ORDER[(k - 4) // 4], slot), which), at(0, to)
            remote(block, block, self.send, self.landing(k), (target, self.view.e)).start()

    def await_(self, k):
        all_landed(self.part(0, None), self.landing(k))

    def await_halves(self):
        all_landed(self.part(pl.ds(0, SIDE), None), self.recv.at[11])

    def finish(self, blocks):
        all_sent(blocks, self.send)


def first_sends(gathers):
    for g in gathers:
        g.start(0, 1)
    for g in gathers:
        g.start(4, 5)


def first_hop(gathers):
    for g in gathers:
        g.await_(0)
        g.start(2, 8, 9)
        g.await_(1)
        g.start(3, 12, 13)


def first_axis_done(gathers):
    for g in gathers:
        g.await_(2)
        g.start(16, 17)


def second_hop_of(gathers, j):
    for g in gathers:
        g.await_(4 + 4 * j)
        g.start(6 + 4 * j)
        g.await_(5 + 4 * j)
        g.start(7 + 4 * j)


def second_hop(gathers):
    for j in range(SIDE):
        second_hop_of(gathers, j)


def second_axis_done(gathers):
    for g in gathers:
        g.await_halves()


def rows_part(ref, begin, length):
    def part(slot, which):
        if which is None:
            return ref.at[slot, pl.ds(begin, length), :]
        return ref.at[slot, pl.ds(begin + which * (length // 2), length // 2), :]

    return part


def mix(
    tok,
    wx,
    wz,
    cw_hbm,
    cb_hbm,
    sw_hbm,
    ss,
    sg_hbm,
    wo,
    extra_loads,
    out,
    tg,
    gw,
    go,
    cw,
    cb,
    sw,
    sg,
    steps,
    acc,
    gate,
    ext,
    tail,
    halo,
    mw,
    keep,
    cum,
    read,
    q0,
    q1,
    q2,
    q3,
    sb,
    st,
    mg,
    ml,
    part,
    pair,
    summed,
    landed,
    leave,
    fin,
    town,
    load_sem,
    tok_send,
    tok_recv,
    w_send,
    w_recv,
    ss_send,
    ss_recv,
    z_send,
    z_recv,
    core_send,
    core_recv,
    gw_send,
    gw_recv,
    go_send,
    go_recv,
    halo_send,
    halo_recv,
    q_send,
    q_recv,
    st_send,
    st_recv,
    mg_send,
    mg_recv,
    pair_send,
    pair_recv,
    sum_send,
    sum_recv,
    fin_send,
    fin_recv,
):
    c, e = lax.axis_index("ctx"), lax.axis_index("exp")
    y, x = c // SIDE, lax.rem(c, SIDE)
    z, core = e // 2, lax.rem(e, 2)
    partner = z * 2 + 1 - core
    rows, width = tok.shape
    lanes = wx.shape[1] // SIDE
    own_rows = out.shape[0]

    def around(value, size):
        return lax.rem(value + size, size)

    def first(ref, count):
        return ref.at[pl.ds(0, count)]

    def in_row(index):
        return y * SIDE + index // 2, z * 2 + lax.rem(index, 2)

    def along_z(d):
        return c, around(z + d, DEPTH) * 2 + core

    def along_y(d):
        return around(y + d, SIDE) * SIDE + x, e

    def along_x(d):
        return y * SIDE + around(x + d, SIDE), e

    spot = x * 2 + core
    spots = 2 * SIDE
    meet = greeting(
        (SIDE, along_x),
        (SIDE, along_y),
        (2, lambda d: along_z(d)),
        (2, lambda d: along_z(-d)),
        (2, lambda d: (c, partner)),
    )

    def columns(block):
        return pl.ds(pl.multiple_of(block * lanes, lanes), lanes)

    mine = columns(x)
    loads = [
        pltpu.make_async_copy(source, place, load_sem.at[i])
        for i, (source, place) in enumerate(
            (
                (tok, tg.at[e, x]),
                (wx.at[:, mine], gw.at[c, :, pl.ds(0, lanes)]),
                (wz.at[:, mine], gw.at[c, :, pl.ds(lanes, lanes)]),
                (ss.at[:, mine], steps.at[x]),
                (cw_hbm.at[:, mine], cw),
                (cb_hbm.at[:, mine], cb),
                (sw_hbm.at[:, mine], sw),
                (sg_hbm.at[:, mine], sg),
                (wo, go.at[y]),
            )
        )
    ]
    for load in loads:
        load.start()
    for load in extra_loads:
        load.start()
    meet()

    for load in loads[:3]:
        load.wait()
    for d in (2, 1, 3):
        remote(tg.at[e, x], tg.at[e, x], tok_send, tok_recv.at[d - 1], along_x(d)).start()
    for d in (1, 3, 2):
        theirs = columns(around(x + d, SIDE))
        for i, weight in enumerate((wx, wz)):
            place = gw.at[c, :, pl.ds(i * lanes, lanes)]
            remote(weight.at[:, theirs], place, w_send, w_recv.at[d - 1], along_x(d)).start()

    def z_part(zz, s, which):
        slot = around(zz, DEPTH) * 2 + core
        if which is None:
            return tg.at[slot, s]
        return tg.at[slot, s, pl.ds(which * (rows // 2), rows // 2), :]

    def z_copy(way, hop, s):
        block = z - (hop - 1) if way == 0 else z + (hop - 1)
        ref = z_part(block, s, None if hop < 4 else way)
        to = around(z + (1 if way == 0 else -1), DEPTH) * 2 + core
        return remote(ref, ref, z_send, z_recv.at[hop - 1, s], (c, to))

    def z_start(hop, s):
        for way in range(2):
            z_copy(way, hop, s).start()

    def core_copy(zz):
        ref = tg.at[zz * 2 + core]
        return remote(ref, ref, core_send, core_recv, (c, partner))

    order = [around(x + d, SIDE) for d in PlaneGather.ORDER]
    weights = PlaneGather(
        rows_part(gw, 0, gw.shape[1]), True, gw_send, gw_recv
    )
    z_start(1, order[0])
    weights.start(4, 5)
    for i, d in ((1, 1), (2, 3), (3, 2)):
        all_landed(tg.at[0, 0], tok_recv.at[d - 1])
        z_start(1, order[i])
    core_copy(z).start()
    for i, d in ((1, 1), (2, 3), (3, 2)):
        all_landed(gw.at[0], w_recv.at[d - 1])
        weights.start(4 + 4 * i, 5 + 4 * i)
    for d in (1, 3, 2):
        theirs = columns(around(x + d, SIDE))
        remote(ss.at[:, theirs], steps.at[x], ss_send, ss_recv, along_x(d)).start()

    def z_hop(hop):
        for s in order:
            if hop < 4:
                all_landed(tg.at[0, pl.ds(0, 2)], z_recv.at[hop - 1, s])
                z_start(hop + 1, s)
            else:
                all_landed(tg.at[0, 0], z_recv.at[hop - 1, s])
        core_copy(around(z - hop, DEPTH)).start()
        if hop < 4:
            core_copy(around(z + hop, DEPTH)).start()

    second_hop_of((weights,), 0)
    z_hop(1)
    second_hop_of((weights,), 1)
    second_hop_of((weights,), 2)
    z_hop(2)
    second_hop_of((weights,), 3)
    z_hop(3)
    second_axis_done((weights,))
    outs = PlaneGather(
        lambda slot, which: go.at[slot // SIDE]
        if which is None
        else go.at[slot // SIDE, pl.ds(which * (go.shape[1] // 2), go.shape[1] // 2), :],
        False,
        go_send,
        go_recv,
    )
    for load in loads[3:]:
        load.wait()
    outs.start(0, 1)
    all_landed(first(steps, SIDE - 1), ss_recv)
    keep[...] = jnp.exp(-jnp.concatenate([steps[s] for s in range(SIDE)], axis=1))
    z_hop(4)

    all_landed(first(tg, DEPTH), core_recv)

    acc[...] = jnp.zeros_like(acc)
    many = SIDE * rows

    @pl.loop(0, EXPS)
    def _(j):
        acc[...] += jnp.dot(tg[j].reshape(many, width), gw[j], preferred_element_type=f32)

    held = halo.shape[0]
    tail[...] = acc[pl.ds(many - held, held), pl.ds(0, lanes)].astype(bf16)

    def halo_copy():
        return remote(tail, halo, halo_send, halo_recv, along_y(1))

    @pl.when(y < SIDE - 1)
    def _():
        halo_copy().start()

    for s in range(SIDE):
        at = pl.ds(s * lanes, lanes)
        here = pl.ds(s * rows, rows)
        ext[pl.ds(held, rows), at] = acc[here, pl.ds(0, lanes)].astype(bf16).astype(f32)
        gate[:, at] = acc[here, pl.ds(lanes, lanes)].astype(bf16).astype(f32)
        if s:
            ext[pl.ds(0, held), at] = ext[pl.ds(rows, held), pl.ds((s - 1) * lanes, lanes)]

    @pl.when(y == 0)
    def _():
        halo[...] = jnp.zeros_like(halo)

    @pl.when(y > 0)
    def _():
        halo_copy().wait_recv()

    ext[pl.ds(0, held), pl.ds(0, lanes)] = halo[...].astype(f32)

    def spread(values):
        return jnp.concatenate([values] * SIDE, axis=1)

    filtered = jnp.broadcast_to(spread(cb[...]), keep.shape)
    for offset in range(CONV):
        begin = held - (CONV - 1) + offset
        tap = spread(cw[pl.ds(offset, 1), :])
        filtered = filtered + tap * ext[pl.ds(begin, rows), :]
    mixer_in = (filtered / (1.0 + jnp.exp(-filtered))).astype(bf16)
    mw[...] = mixer_in.astype(f32)

    for s in range(SIDE):
        both = lax.dot_general(
            sw[...],
            mixer_in[:, s * lanes : (s + 1) * lanes],
            (((1,), (1,)), ((), ())),
            preferred_element_type=f32,
        )
        q0[2 * s] = both[:STATE]
        q0[2 * s + 1] = both[STATE:]

    def to_sum(source, there):
        return remote(
            q0.at[there], q1.at[source], q_send.at[0], q_recv.at[0], in_row(there)
        )

    def z_sum(d, source):
        return remote(q2.at[source], q2.at[source], q_send.at[1], q_recv.at[1], along_z(d))

    def to_share(source, there):
        return remote(
            q3.at[source], q3.at[source], q_send.at[2], q_recv.at[2], in_row(there)
        )

    @pl.loop(1, spots)
    def _(d):
        to_sum(spot, around(spot + d, spots)).start()

    q1[spot] = q0[spot]
    outs.await_(0)
    outs.start(2)
    outs.await_(1)
    outs.start(3)

    picked = lax.broadcasted_iota(jnp.int32, (own_rows, rows), 1) == (
        lax.broadcasted_iota(jnp.int32, (own_rows, rows), 0) + e * own_rows
    )
    picker = picked.astype(f32).astype(bf16)

    @pl.loop(0, EXPS)
    def _(j):
        town[j] = jnp.dot(picker, tg[j, x], preferred_element_type=f32)

    all_landed(first(q1, spots - 1), q_recv.at[0])

    total = q1[0]
    for j in range(1, spots):
        total = total + q1[j]
    q2[z] = total

    @pl.loop(1, DEPTH)
    def _(d):
        z_sum(d, z).start()

    all_landed(first(q2, DEPTH - 1), q_recv.at[1])

    total = q2[0]
    for j in range(1, DEPTH):
        total = total + q2[j]
    q3[spot] = total

    @pl.loop(1, spots)
    def _(d):
        to_share(spot, around(spot + d, spots)).start()

    all_landed(first(q3, spots - 1), q_recv.at[2])

    chunks = rows // CHUNK
    for k in range(2):
        for s in range(SIDE):
            vectors = q3[2 * s + k]
            for j in range(chunks):
                sb[j, pl.ds(k * STATE, STATE), pl.ds(s * CHUNK, CHUNK)] = vectors[
                    :, j * CHUNK : (j + 1) * CHUNK
                ]

    def advance(j, carry):
        state, decay = carry
        vectors = sb[j]
        first = pl.multiple_of(j * CHUNK, CHUNK)
        keeps, inputs = keep[pl.ds(first, CHUNK), :], mw[pl.ds(first, CHUNK), :]

        def vector(begin, i):
            picks = [
                jnp.broadcast_to(
                    vectors[begin : begin + STATE, s * CHUNK + i : s * CHUNK + i + 1],
                    (STATE, lanes),
                )
                for s in range(SIDE)
            ]
            return jnp.concatenate(picks, axis=1)

        for i in range(CHUNK):
            kept = keeps[i : i + 1, :]
            state = kept * state + inputs[i : i + 1, :] * vector(0, i)
            decay = decay * kept
            read[pl.ds(first + i, 1), :] = jnp.sum(
                vector(STATE, i) * state, axis=0, keepdims=True
            )
            cum[pl.ds(first + i, 1), :] = decay
        return state, decay

    wide = SIDE * lanes
    state, decay = lax.fori_loop(
        0, chunks, advance, (jnp.zeros((STATE, wide), f32), jnp.ones((1, wide), f32))
    )

    ends = [state[:, s * lanes : (s + 1) * lanes] for s in range(SIDE)]
    keeps = [decay[:, s * lanes : (s + 1) * lanes] for s in range(SIDE)]
    row_end, row_keep = ends[0], keeps[0]
    for s in range(1, SIDE):
        row_end, row_keep = keeps[s] * row_end + ends[s], keeps[s] * row_keep
    st[y, pl.ds(0, STATE), :] = row_end
    st[y, pl.ds(STATE, 8), :] = jnp.broadcast_to(row_keep, (8, lanes))

    def st_copy(d, slot):
        return remote(st.at[slot], st.at[slot], st_send.at[d], st_recv.at[d], along_y(d))

    @pl.loop(1, SIDE - y)
    def _(d):
        st_copy(d, y).start()

    gated = gate[...] / (1.0 + jnp.exp(-gate[...]))
    inside = read[...] + spread(sg[...]) * mw[...]

    def enter(source, entering):
        st_copy(y - source, source).wait_recv()
        return st[source, pl.ds(STATE, 1), :] * entering + st[source, pl.ds(0, STATE), :]

    entering = lax.fori_loop(0, y, enter, jnp.zeros((STATE, lanes), f32))
    carried = []
    for s in range(SIDE):
        carried.append(
            lax.dot_general(
                q3[2 * s + 1],
                entering,
                (((0,), (0,)), ((), ())),
                preferred_element_type=f32,
                precision=precise,
            )
        )
        entering = keeps[s] * entering + ends[s]
    mixed = (inside + cum[...] * jnp.concatenate(carried, axis=1)) * gated
    for s in range(SIDE):
        mg[x, s] = mixed[:, s * lanes : (s + 1) * lanes].astype(bf16)

    for d in (2, 1, 3):
        remote(mg.at[x], mg.at[x], mg_send, mg_recv, along_x(d)).start()
    outs.await_(2)
    all_landed(first(mg, SIDE - 1), mg_recv)
    for s in range(SIDE):
        ml[:, pl.ds(s * lanes, lanes)] = mg[s].reshape(many, lanes)

    block_columns = go.shape[2]
    pieces = [pl.ds(h * block_columns, block_columns) for h in range(SIDE)]

    def pair_copy(h):
        return remote(
            part.at[1 - core, :, :, :, pieces[h]],
            pair.at[:, :, :, pieces[h]],
            pair_send.at[h],
            pair_recv.at[h],
            (c, partner),
        )

    def sum_copy(h, d, there, source):
        return remote(
            summed.at[there, :, :, pieces[h]],
            landed.at[source, :, :, pieces[h]],
            sum_send.at[h],
            sum_recv.at[h],
            along_z(d),
        )

    def both_cores(h, there):
        at = pieces[h]
        return part[core, there, :, :, at].astype(f32) + pair[there, :, :, at].astype(f32)

    for h in range(SIDE):
        block = jnp.dot(ml[...], go[h], preferred_element_type=f32)
        for i in range(EXPS):
            for s in range(SIDE):
                begin = s * rows + i * own_rows
                part[i % 2, i // 2, s, :, pieces[h]] = block[begin : begin + own_rows].astype(bf16)
        pair_copy(h).start()
    for h in range(SIDE):
        pair_copy(h).wait_recv()

        @pl.loop(1, DEPTH)
        def _(d):
            there = around(z + d, DEPTH)
            summed[there, :, :, pieces[h]] = both_cores(h, there).astype(bf16)
            sum_copy(h, d, there, z).start()

    for h in range(SIDE):

        def collect(d, total):
            return total + landed[around(z - d, DEPTH), :, :, pieces[h]].astype(f32)

        all_landed(landed.at[pl.ds(0, DEPTH - 1), :, :, pieces[h]], sum_recv.at[h])
        total = lax.fori_loop(1, DEPTH, collect, both_cores(h, z))
        leave[:, :, pieces[h]] = total.astype(bf16)

    def fin_copy(there, source):
        return remote(
            leave.at[there], fin.at[source], fin_send, fin_recv, (y * SIDE + there, e)
        )

    for d in (1, 3, 2):
        fin_copy(around(x + d, SIDE), x).start()
    fin[x] = leave[x]
    all_landed(first(fin, SIDE - 1), fin_recv)
    for i in range(SIDE):
        for s in range(SIDE):
            block = i * SIDE + s
            term = fin[s, :, pl.ds(i * block_columns, block_columns)].astype(f32)
            out[:, pl.ds(block * width, width)] = (town[block] + term).astype(bf16)

    all_sent(tg.at[0, pl.ds(0, SIDE - 1)], tok_send)
    all_sent(first(gw, SIDE - 1), w_send)
    all_sent(first(steps, SIDE - 1), ss_send)
    all_sent(first(tg, DEPTH - 1), z_send)
    all_sent(first(tg, DEPTH), core_send)
    weights.finish(first(gw, 12))
    outs.finish(first(go, SIDE - 1))
    all_sent(first(mg, SIDE - 1), mg_send)
    all_sent(first(q0, spots - 1), q_send.at[0])
    all_sent(first(q2, DEPTH - 1), q_send.at[1])
    all_sent(first(q3, spots - 1), q_send.at[2])
    for h in range(SIDE):
        all_sent(summed.at[pl.ds(0, DEPTH - 1), :, :, pieces[h]], sum_send.at[h])
        pair_copy(h).wait_send()
    all_sent(first(leave, SIDE - 1), fin_send)

    @pl.when(y < SIDE - 1)
    def _():
        halo_copy().wait_send()

    @pl.loop(1, SIDE - y)
    def _(d):
        st_copy(d, y).wait_send()


def mix_scratch(rows, width, depth, inner):
    lanes = inner // SIDE
    model = width * EXPS
    own = rows // EXPS
    dma = pltpu.SemaphoreType.DMA
    vmem = pltpu.VMEM
    wide = vmem((rows, inner), f32)
    spread = (DEPTH, SIDE, own, model // SIDE)
    vectors = vmem((2 * SIDE, STATE, rows), f32)
    return [
        vmem((EXPS, SIDE, rows, width), bf16),
        vmem((PLANE, depth, 2 * lanes), bf16),
        vmem((SIDE, inner, width), bf16),
        vmem((CONV, lanes), f32),
        vmem((1, lanes), f32),
        vmem((2 * STATE, lanes), bf16),
        vmem((1, lanes), f32),
        vmem((SIDE, rows, lanes), f32),
        vmem((SIDE * rows, 2 * lanes), f32),
        wide,
        vmem((rows + 16, inner), f32),
        vmem((16, lanes), bf16),
        vmem((16, lanes), bf16),
        wide,
        wide,
        wide,
        wide,
        vectors,
        vectors,
        vmem((DEPTH, STATE, rows), f32),
        vectors,
        vmem((rows // CHUNK, 2 * STATE, 128), f32),
        vmem((SIDE, STATE + 8, lanes), f32),
        vmem((SIDE, SIDE, rows, lanes), bf16),
        vmem((SIDE * rows, inner), bf16),
        vmem((2, *spread), bf16),
        vmem(spread, bf16),
        vmem(spread, bf16),
        vmem(spread, bf16),
        vmem(spread[1:], bf16),
        vmem(spread[1:], bf16),
        vmem((EXPS, own, width), f32),
        dma((9,)),
        dma,
        dma((3,)),
        dma,
        dma((3,)),
        dma,
        dma,
        dma,
        dma((4, SIDE)),
        dma,
        dma,
        dma,
        dma((12,)),
        dma,
        dma((3,)),
        dma,
        dma,
        dma((3,)),
        dma((3,)),
        dma((SIDE,)),
        dma((SIDE,)),
        dma,
        dma,
        dma((SIDE,)),
        dma((SIDE,)),
        dma((SIDE,)),
        dma((SIDE,)),
        dma,
        dma,
    ]


class PlaneReduce:
    ORDER = (2, -1, 1, 0)

    def __init__(self, part, late, x_first, send, recv):
        self.view, self.part, self.late = PlaneView(x_first), part, late
        self.send, self.recv = send, recv

    def mine(self, j, step, which):
        at = self.view.at
        return self.part(at(self.ORDER[j], step) if j < 4 else at(step, 0), which)

    def start(self, k):
        j, kind = k // 4, k % 4
        step, which, to = ((2, 0, 1), (2, 1, -1), (1, None, 1), (-1, None, -1))[kind]
        target = self.view.at(0, to) if j < 4 else self.view.at(to, 0)
        source, place = self.mine(j, step, which), self.late(k, which)
        remote(source, place, self.send, self.recv.at[k // 2], (target, self.view.e)).start()

    def far(self, j):
        self.start(4 * j)
        self.start(4 * j + 1)

    def near(self, j):
        all_landed(self.late(4 * j, None), self.recv.at[2 * j])
        for kind, step in ((0, 1), (1, -1)):
            mine, came = self.mine(j, step, kind), self.late(4 * j + kind, kind)
            mine[...] = (mine[...].astype(f32) + came[...].astype(f32)).astype(bf16)
            self.start(4 * j + 2 + kind)

    def close(self, j):
        all_landed(self.late(pl.ds(4 * j + 2, 2), None), self.recv.at[2 * j + 1])
        mine, first, second = self.mine(j, 0, None), self.late(4 * j + 2, None), self.late(4 * j + 3, None)
        total = first[...].astype(f32) + second[...].astype(f32)
        mine[...] = (mine[...].astype(f32) + total).astype(bf16)

    def finish(self):
        all_sent(self.part(pl.ds(0, 15), None), self.send)


def chunk_part(ref, row, rows, column, columns):
    def part(slot, which):
        if which is None:
            return ref.at[slot, pl.ds(row, rows), pl.ds(column, columns)]
        half = columns // 2
        return ref.at[slot, pl.ds(row, rows), pl.ds(column + which * half, half)]

    return part


def route(residual, norm_gain, router, ids):
    stream = residual[...].astype(f32)
    scale = lax.rsqrt(jnp.mean(stream * stream, axis=1, keepdims=True) + 1e-05)
    normed = (stream * scale * norm_gain[...]).astype(bf16)
    logits = lax.dot_general(
        router[...], normed, (((1,), (1,)), ((), ())), preferred_element_type=f32
    )
    experts, rows = logits.shape
    expert = lax.broadcasted_iota(jnp.int32, (experts, rows), 0)
    slot = lax.broadcasted_iota(jnp.int32, (experts * CAP, rows), 0).astype(f32)
    before = lax.broadcasted_iota(jnp.int32, (rows, rows), 0) < lax.broadcasted_iota(
        jnp.int32, (rows, rows), 1
    )
    named = [ids[pl.ds(k, 1), :] for k in range(TOP)]
    hits = [(expert == one).astype(f32) for one in named]
    earlier = jnp.dot(
        hits[0] + hits[1], before.astype(f32), preferred_element_type=f32, precision=precise
    )
    picked = [jnp.sum(hit * logits, axis=0, keepdims=True) for hit in hits]
    selector = jnp.zeros(slot.shape, f32)
    combine = jnp.zeros(slot.shape, f32)
    for k in range(TOP):
        rank = jnp.sum(hits[k] * earlier, axis=0, keepdims=True)
        placed = (slot == named[k].astype(f32) * CAP + rank).astype(f32)
        share = 1.0 / (1.0 + jnp.exp(picked[1 - k] - picked[k]))
        selector = selector + placed
        combine = combine + placed * share
    return normed, selector.astype(bf16), combine


def run_experts(
    residual,
    norm_gain,
    router,
    ids,
    loads,
    out,
    wg,
    wu,
    wd,
    give,
    take,
    back,
    ret,
    packed,
    rows_in,
    acc_g,
    acc_u,
    sums,
    late,
    out_send,
    out_recv,
    back_send,
    back_recv,
    ag_send,
    ag_recv,
    rs_send,
    rs_recv,
):
    c, e = lax.axis_index("ctx"), lax.axis_index("exp")
    slots, model = packed.shape
    turned = (((1,), (1,)), ((), ()))

    for load in loads[3:]:
        load.wait()
    normed, selector, combine = route(residual, norm_gain, router, ids)
    packed[...] = jnp.dot(selector, normed, preferred_element_type=f32)
    for j in range(EXPS):
        give[j] = packed[pl.ds(j * CAP, CAP), :].astype(bf16)
    take[e] = give[e]

    def out_copy(there, source):
        return remote(
            give.at[there], take.at[source], out_send, out_recv.at[source // (EXPS // 2)], (c, there)
        )

    @pl.loop(1, EXPS)
    def _(d):
        out_copy(lax.rem(e + d, EXPS), e).start()

    half_rows, half_model = slots // 2, model // 2
    gathers, reduces = [], []
    for i in range(2):
        row = i * half_rows
        gathers.append(
            [
                PlaneGather(
                    chunk_part(rows_in, row, half_rows, h * half_model, half_model),
                    h == 0,
                    ag_send.at[i, h],
                    ag_recv.at[i, h],
                )
                for h in range(2)
            ]
        )

        def landing(i, h):
            def at(k, which):
                if which is None:
                    return late.at[i, h, k]
                return late.at[i, h, k, :, pl.ds(which * (half_model // 2), half_model // 2)]

            return at

        reduces.append(
            [
                PlaneReduce(
                    chunk_part(sums, row, half_rows, h * half_model, half_model),
                    landing(i, h),
                    h == 0,
                    rs_send.at[i, h],
                    rs_recv.at[i, h],
                )
                for h in range(2)
            ]
        )

    def collect(i):
        first = i * (EXPS // 2)

        @pl.when(e // (EXPS // 2) == i)
        def _():
            all_landed(take.at[pl.ds(0, EXPS // 2 - 1)], out_recv.at[i])

        @pl.when(e // (EXPS // 2) != i)
        def _():
            all_landed(take.at[pl.ds(0, EXPS // 2)], out_recv.at[i])

        for j in range(first, first + EXPS // 2):
            packed[pl.ds(j * CAP, CAP), :] = take[j].astype(f32)
        at = pl.ds(i * half_rows, half_rows)
        rows_in[c, at, :] = packed[at, :].astype(bf16)

    step = 512
    many = PLANE * half_rows

    def gate_up(i, begin, end):
        @pl.loop(begin, end)
        def _(k):
            at = pl.ds(pl.multiple_of(k * step, step), step)
            block = rows_in[:, pl.ds(i * half_rows, half_rows), at].reshape(many, step)
            acc_g[i] += lax.dot_general(block, wg[:, at], turned, preferred_element_type=f32)
            acc_u[i] += lax.dot_general(block, wu[:, at], turned, preferred_element_type=f32)

    def hidden_of(i):
        gate = acc_g[i]
        return ((gate / (1.0 + jnp.exp(-gate))) * acc_u[i]).astype(bf16)

    def down(i, hidden, begin, end):
        @pl.loop(begin, end)
        def _(k):
            at = pl.ds(pl.multiple_of(k * step, step), step)
            block = jnp.dot(hidden, wd[:, at], preferred_element_type=f32)
            sums[:, pl.ds(i * half_rows, half_rows), at] = block.astype(bf16).reshape(
                PLANE, half_rows, step
            )

    def give_back(i):
        for r in reduces[i]:
            r.close(4)
        packed[pl.ds(i * half_rows, half_rows), :] = sums[
            c, pl.ds(i * half_rows, half_rows), :
        ].astype(f32)
        first = i * (EXPS // 2)
        for j in range(first, first + EXPS // 2):
            back[j] = packed[pl.ds(j * CAP, CAP), :].astype(bf16)

        @pl.loop(first, first + EXPS // 2)
        def _(j):
            @pl.when(j != e)
            def _():
                back_copy(j, e).start()

            @pl.when(j == e)
            def _():
                ret[e] = back[e]

    def back_copy(there, source):
        return remote(
            back.at[there], ret.at[source], back_send, back_recv, (c, there)
        )

    first, second = gathers
    collect(0)
    first_sends(first)
    collect(1)
    first_sends(second)
    acc_g[...] = jnp.zeros_like(acc_g)
    acc_u[...] = jnp.zeros_like(acc_u)
    first_hop(first)
    first_hop(second)
    first_axis_done(first)
    first_axis_done(second)
    second_hop(first)
    second_axis_done(first)
    for load in loads[:3]:
        load.wait()
    steps = model // step
    for j in range(SIDE):
        gate_up(0, j * (steps // SIDE), (j + 1) * (steps // SIDE))
        second_hop_of(second, j)
    hidden = hidden_of(0)
    down(0, hidden, 0, steps)
    for j in range(SIDE):
        for r in reduces[0]:
            r.far(j)
    second_axis_done(second)
    for j in range(SIDE):
        gate_up(1, j * (steps // SIDE), (j + 1) * (steps // SIDE))
        for r in reduces[0]:
            r.near(j)
    hidden = hidden_of(1)
    down(1, hidden, 0, steps)
    for j in range(SIDE):
        for r in reduces[1]:
            r.far(j)
    for j in range(SIDE):
        for r in reduces[0]:
            r.close(j)
            if j == 0:
                r.far(4)
    for j in range(SIDE):
        for r in reduces[1]:
            r.near(j)
    for r in reduces[0]:
        r.near(4)
    for j in range(SIDE):
        for r in reduces[1]:
            r.close(j)
            if j == 0:
                r.far(4)
    give_back(0)
    for r in reduces[1]:
        r.near(4)
    give_back(1)

    all_landed(ret.at[pl.ds(0, EXPS - 1)], back_recv)
    for j in range(EXPS):
        packed[pl.ds(j * CAP, CAP), :] = ret[j].astype(f32)
    moe = lax.dot_general(
        combine,
        packed[...],
        (((0,), (0,)), ((), ())),
        preferred_element_type=f32,
        precision=precise,
    )
    out[...] = (residual[...].astype(f32) + moe).astype(bf16)

    for pair in gathers:
        for g in pair:
            g.finish(g.part(pl.ds(0, 15), None))
    for pair in reduces:
        for r in pair:
            r.finish()
    all_sent(give.at[pl.ds(0, EXPS - 1)], out_send)
    all_sent(back.at[pl.ds(0, EXPS - 1)], back_send)


def expert_scratch(units, model):
    slots = EXPS * CAP
    dma = pltpu.SemaphoreType.DMA
    vmem = pltpu.VMEM
    weight = vmem((units, model), bf16)
    pairs = vmem((EXPS, CAP, model), bf16)
    return [
        weight,
        weight,
        weight,
        pairs,
        pairs,
        pairs,
        pairs,
        vmem((slots, model), f32),
        vmem((PLANE, slots, model), bf16),
        vmem((2, PLANE * slots // 2, units), f32),
        vmem((2, PLANE * slots // 2, units), f32),
        vmem((PLANE, slots, model), bf16),
        vmem((2, 2, 20, slots // 2, model // 2), bf16),
        dma,
        dma((2,)),
        dma,
        dma,
        dma((2, 2)),
        dma((2, 2, 12)),
        dma((2, 2)),
        dma((2, 2, 10)),
    ]


def layer_kernel(mix_count, *refs):
    mix_ins, (gain_hbm, router_hbm, wg_hbm, wu_hbm, wd_hbm, ids_hbm), out = refs[:9], refs[9:15], refs[15]
    residual, gain, router, ids, load_sem = refs[16:21]
    mix_refs, expert_refs = refs[21 : 21 + mix_count], refs[21 + mix_count :]
    loads = [
        pltpu.make_async_copy(source, place, load_sem.at[i])
        for i, (source, place) in enumerate(
            zip(
                (wg_hbm, wu_hbm, wd_hbm, gain_hbm, router_hbm, ids_hbm),
                (*expert_refs[:3], gain, router, ids),
                strict=True,
            )
        )
    ]
    mix(*mix_ins, loads, residual, *mix_refs)
    run_experts(residual, gain, router, ids, loads, out, *expert_refs)


def local(
    tokens,
    input_weight,
    gate_weight,
    conv_weight,
    conv_bias,
    state_weight,
    step_size,
    skip_gain,
    output_weight,
    norm_gain,
    router_weight,
    expert_gate,
    expert_up,
    expert_down,
    expert_ids,
):
    own, model = expert_ids.shape[0], norm_gain.shape[0]
    units, experts = expert_gate.shape[1], router_weight.shape[1]
    scratch = mix_scratch(*tokens.shape, *input_weight.shape)
    vmem = pltpu.VMEM
    return pl.pallas_call(
        functools.partial(layer_kernel, len(scratch)),
        out_shape=jax.ShapeDtypeStruct((own, model), bf16),
        in_specs=[pl.BlockSpec(memory_space=pltpu.HBM)] * 15,
        out_specs=pl.BlockSpec(memory_space=pltpu.VMEM),
        scratch_shapes=[
            vmem((own, model), bf16),
            vmem((1, model), f32),
            vmem((experts, model), bf16),
            vmem((TOP, own), jnp.int32),
            pltpu.SemaphoreType.DMA((6,)),
            *scratch,
            *expert_scratch(units, model),
        ],
        compiler_params=pltpu.CompilerParams(
            collective_id=0, has_side_effects=True, vmem_limit_bytes=62 << 20
        ),
        name="layer",
    )(
        tokens,
        input_weight,
        gate_weight,
        conv_weight,
        conv_bias.reshape(1, -1),
        state_weight.T,
        step_size,
        skip_gain.reshape(1, -1),
        output_weight,
        norm_gain.reshape(1, -1),
        router_weight.T,
        expert_gate[0],
        expert_up[0],
        expert_down[0],
        expert_ids.T,
    )


def solution(mesh):
    in_specs = (
        P("ctx", "exp"),
        P("ctx", "exp"),
        P("ctx", "exp"),
        P(None, "exp"),
        P("exp"),
        P("exp", None),
        P("ctx", "exp"),
        P("exp"),
        P("exp", "ctx"),
        P(),
        P(),
        P("exp", "ctx", None),
        P("exp", "ctx", None),
        P("exp", "ctx", None),
        P(("ctx", "exp"), None),
    )
    out_specs = P(("ctx", "exp"), None)
    return jax.shard_map(local, mesh=mesh, in_specs=in_specs, out_specs=out_specs, check_vma=False)
```
